32 devices in a mesh: stn: 8 (over z, x), chan: 4 (over y, core).
Axes of the slice: x: 2, y: 2, z: 4, core: 2. Of those that a mesh axis runs over, the one named last changes fastest.
Arguments:
- samples: bfloat16 [64, 17, 2, 8192], P(('stn', 'chan')), may hold values from -6 to 6
- keeper: int32 [8, 8], replicated, may hold values from 0 to 1, as said below
Outputs:
- visibilities: bfloat16 [64, 2, 4096, 40], P('stn', None, 'chan')
The draws below stay inside these ranges and needn't reach their ends.
Inputs may be any that keep to these rules, and one draw needn't show every extreme that they name: keeper[g, g] is 1; for g != h with d = (g - h) mod 8: keeper[g, h] is 1 where 0 < d < 4, 0 where d > 4, and at d = 4 exactly one of keeper[g, h] and keeper[h, g] is 1, which one drawn for each such pair; half of the rows hold 5 ones, the others 5 - 1.
All inputs are finite; a program needn't handle non-finite values.
Results may differ from the reference program's by a relative error of at most 0.0077.
Values may be sent and summed in bfloat16 or wider, within the bound.
A program may use at most 192 MiB of HBM per device.

```python
import math
import jax
import jax.numpy as jnp
from jax import lax

NFFT = 8192
TAPS = 16
STN_DEV = 1
CH_WIN = 1024
DFT_BLOCK = 256
FRAMES = 2
FRAMES_IN = 17
GROUPS = 8
INPUTS = 64
N_STN = 8
N_CHAN = 4


def draw_keeper(key, part):
    middle = GROUPS // 2
    coins = jax.random.randint(jax.random.fold_in(key, 11), (middle,), 0, 2).astype(jnp.int32)
    first = jnp.arange(GROUPS, dtype=jnp.int32)[:, None]
    second = jnp.arange(GROUPS, dtype=jnp.int32)[None, :]
    distance = (first - second) % GROUPS
    coin_row = jnp.take(coins, first % middle)
    lower_wins = (first < second) == (coin_row == 0)
    kept = (distance == 0) | (distance >= 1) & (distance < middle) | (distance == middle) & lower_wins
    return kept.astype(jnp.int32)


def block_levels(rng, dims, pieces, low, largest):
    def one(axis_at, blocks):
        heights = jax.random.uniform(jax.random.fold_in(jax.random.fold_in(rng, 6), axis_at), (blocks,), jnp.float32, low / len(pieces), largest / len(pieces))
        return jnp.repeat(jnp.exp(heights), dims[axis_at] // blocks).reshape((-1,) + (1,) * (len(dims) - axis_at - 1))

    loudness = one(*pieces[0])
    for cut in pieces[1:]:
        loudness = loudness * one(*cut)
    return loudness


def bell_draw(stream_key, dims, scale, limit, split=(), kind=jnp.bfloat16):
    factor_of = block_levels(stream_key, dims, split, -0.22, 0.18) if split else 1.0
    entries = jax.random.normal(stream_key, dims, jnp.float32) * scale * factor_of
    return jnp.minimum(jnp.maximum(entries, -limit), limit).astype(kind)


def setup_inputs(seed: int = 0) -> dict:
    key_list = jax.random.split(jax.random.key(seed), 3)
    return {
        "samples": bell_draw(key_list[0], (INPUTS, FRAMES_IN, 2, NFFT), 1.0, 6.0, ((0, 32),)),
        "keeper": draw_keeper(jax.random.fold_in(key_list[2], 71), 0),
    }


def taps_table():
    pos = jnp.arange(TAPS * NFFT).astype(jnp.float32)
    shifted = (pos + 0.5) / NFFT - TAPS / 2.0
    window = 0.5 - 0.5 * jnp.cos(2.0 * math.pi * (pos + 0.5) / (TAPS * NFFT))
    return (jnp.sinc(shifted) * window).reshape(TAPS, NFFT)

def twiddles(width):
    index_n = jnp.arange(NFFT, dtype=jnp.int32)[:, None]
    index_k = jnp.arange(width, dtype=jnp.int32)[None, :]
    phase = (index_n * index_k % NFFT).astype(jnp.float32) * (2.0 * math.pi / NFFT)
    cosines = jnp.cos(phase).astype(jnp.bfloat16)
    sines = jnp.sin(phase).astype(jnp.bfloat16)
    upper = jnp.concatenate([cosines, -sines], axis=1)
    lower = jnp.concatenate([sines, cosines], axis=1)
    return jnp.concatenate([upper, lower], axis=0)

def rotations(ch_tot, width):
    blocks = ch_tot // width
    index_n = jnp.arange(NFFT, dtype=jnp.int32)[None, :]
    index_b = jnp.arange(blocks, dtype=jnp.int32)[:, None]
    phase = (index_n * index_b * width % NFFT).astype(jnp.float32) * (2.0 * math.pi / NFFT)
    return (jnp.cos(phase), jnp.sin(phase))

def channelise(block, taps, table, cos_rot, sin_rot, ch_tot):
    frames = block.shape[1] - TAPS + 1
    count = block.shape[0]
    width = table.shape[1] // 2
    blocks = ch_tot // width
    total = taps[0] * block[:, 0:frames].astype(jnp.float32)
    for tap in range(1, TAPS):
        total = total + taps[tap] * block[:, tap:tap + frames].astype(jnp.float32)
    real_part = total[:, :, 0][None]
    imag_part = total[:, :, 1][None]
    cosine = cos_rot[:, None, None, :]
    sine = sin_rot[:, None, None, :]
    rot_real = real_part * cosine + imag_part * sine
    rot_imag = imag_part * cosine - real_part * sine
    lhs = jnp.stack([rot_real, rot_imag], axis=3).astype(jnp.bfloat16)
    lhs = lhs.reshape(blocks * count * frames, 2 * NFFT)
    spectrum = jnp.dot(lhs, table, preferred_element_type=jnp.float32) * (1.0 / math.sqrt(NFFT))
    spectrum = spectrum.astype(jnp.bfloat16).reshape(blocks, count, frames, 2, width)
    spectrum = jnp.transpose(spectrum, (1, 0, 4, 3, 2))
    return spectrum.reshape(count, ch_tot, 2, frames)

def correlate(own, others, frames):
    half = others.shape[2] // 2
    turned = jnp.concatenate([-others[:, :, half:], others[:, :, :half]], axis=2)
    rhs = jnp.concatenate([others, turned], axis=0)
    product = lax.dot_general(own.astype(jnp.float32), rhs.astype(jnp.float32), (((2,), (2,)), ((1,), (1,))))
    rows = others.shape[0]
    product = product.reshape(product.shape[0], product.shape[1], 2, rows)
    return jnp.transpose(product, (1, 2, 0, 3)) / frames

def slot_table(keep_rows, keep_slots):
    ranking = (jnp.cumsum(keep_rows, axis=1) - 1).astype(jnp.int32)
    slot_index = jnp.arange(keep_slots, dtype=jnp.int32)
    matched = (keep_rows[:, :, None] == 1) & (ranking[:, :, None] == slot_index[None, None, :])
    column_ids = jnp.arange(keep_rows.shape[1], dtype=jnp.int32)
    slot_column = lax.optimization_barrier(jnp.sum(jnp.where(matched, column_ids[None, :, None], 0), axis=1)).astype(jnp.int32)
    filled = jnp.any(matched, axis=1)
    return (slot_column, filled)

def reference(samples, keeper):
    ch_tot = CH_WIN * N_CHAN
    inputs = samples.shape[0]
    group_in = 2 * STN_DEV * N_CHAN
    keep_slots = N_STN // 2 + 1
    taps = taps_table()
    table = twiddles(DFT_BLOCK)
    cos_rot, sin_rot = rotations(ch_tot, DFT_BLOCK)
    per_block = 2 * STN_DEV
    blocks = samples.reshape(inputs // per_block, per_block, FRAMES_IN, 2, NFFT)
    spectra = lax.map(lambda block: channelise(block, taps, table, cos_rot, sin_rot, ch_tot), blocks)
    spectra = spectra.reshape(inputs, ch_tot, 2 * FRAMES)
    slot_column, filled = slot_table(keeper, keep_slots)
    span_ch = 16

    def one_step(step, result):
        start = (step * span_ch).astype(jnp.int32)
        part = lax.dynamic_slice_in_dim(spectra, start, span_ch, 1)
        tile = correlate(part, part, FRAMES)
        tile = tile.reshape(N_STN, group_in, 2, span_ch, N_STN, group_in)
        picked = jnp.take_along_axis(tile, slot_column[:, None, None, None, :, None], axis=4)
        picked = jnp.where(filled[:, None, None, None, :, None], picked, jnp.zeros((), jnp.float32))
        picked = picked.reshape(inputs, 2, span_ch, keep_slots * group_in).astype(jnp.bfloat16)
        return lax.dynamic_update_slice_in_dim(result, picked, start, 2)
    result = jnp.zeros((inputs, 2, ch_tot, keep_slots * group_in), jnp.bfloat16)
    return lax.fori_loop(0, ch_tot // span_ch, one_step, result)
```

```python
import math

import jax
import jax.numpy as jnp
import numpy as np
from jax import lax
from jax.experimental import pallas as pl
from jax.experimental.pallas import tpu as pltpu
from jax.sharding import PartitionSpec as P

TAPS = 16
LANES = 128
CH_WIN = 1024
HIGH = lax.Precision.HIGHEST
MESH = pl.DeviceIdType.MESH
VMEM_LIMIT = 24 << 20
CHUNKS = 4


def tables(nfft, n_k2):
    n_1 = nfft // LANES
    pos = np.arange(TAPS * nfft, dtype=np.float64)
    window = 0.5 - 0.5 * np.cos(2.0 * np.pi * (pos + 0.5) / (TAPS * nfft))
    taps = np.sinc((pos + 0.5) / nfft - TAPS / 2.0) * window
    taps = np.repeat(taps.reshape(TAPS, n_1, LANES), 2, axis=1)
    k_1 = np.arange(n_1)
    n_2 = np.arange(LANES)
    angle = 2.0 * np.pi * (k_1[:, None] * k_1[None, :] % n_1) / n_1
    cosine, sine = np.cos(angle), np.sin(angle)
    first = np.zeros((2, n_1, n_1, 2))
    first[0, :, :, 0] = cosine
    first[0, :, :, 1] = sine
    first[1, :, :, 0] = -sine
    first[1, :, :, 1] = cosine
    first = first.reshape(2 * n_1, 2 * n_1)
    angle = 2.0 * np.pi * (n_2[:, None] * k_1[None, :] % nfft) / nfft
    scale = 1.0 / math.sqrt(nfft)
    turn_c = np.concatenate([np.cos(angle), np.cos(angle)], axis=1) * scale
    turn_s = np.concatenate([np.sin(angle), -np.sin(angle)], axis=1) * scale
    k_2 = np.concatenate([np.arange(0, n_k2, 2), np.arange(1, n_k2, 2)])
    angle = 2.0 * np.pi * (k_2[:, None] * n_2[None, :] % LANES) / LANES
    second = np.concatenate([np.cos(angle), np.sin(angle)], axis=1)
    return [np.asarray(a, np.float32) for a in (taps, first, turn_c, turn_s, second)]


def filter_rows(x_ref, taps_ref, held, first_row, rows, inputs, frames):
    chunk = 16
    for start in range(first_row, first_row + rows, chunk):
        part = slice(start, start + chunk)
        for i in range(inputs):
            totals = [None] * frames
            for step in range(TAPS + frames - 1):
                value = x_ref[i, step, part, :].astype(jnp.float32)
                for f in range(frames):
                    if 0 <= step - f < TAPS:
                        term = value * taps_ref[step - f, part, :]
                        totals[f] = term if totals[f] is None else totals[f] + term
            for f in range(frames):
                seq = i * frames + f
                held[part, seq * LANES : (seq + 1) * LANES] = totals[f]


def transform(held, first_ref, turn_c_ref, turn_s_ref, second_ref, seqs):
    half = LANES // 2
    stage = jnp.dot(first_ref[...], held[...], precision=HIGH, preferred_element_type=jnp.float32)
    lane = lax.broadcasted_iota(jnp.int32, (LANES, LANES), 1)
    sign = jnp.where(lane < half, 1.0, -1.0)
    tops, lows = [], []
    for seq in range(seqs):
        turned = stage[:, seq * LANES : (seq + 1) * LANES].T
        turned = turned * turn_c_ref[...] + pltpu.roll(turned, half, 1) * turn_s_ref[...]
        tops.append(turned)
        lows.append(pltpu.roll(turned, half, 1) * sign)
    rhs = jnp.concatenate([jnp.concatenate(tops, axis=1), jnp.concatenate(lows, axis=1)], axis=0)
    spectra = jnp.dot(second_ref[...], rhs, precision=HIGH, preferred_element_type=jnp.float32)
    tiles = spectra.shape[0] // 2
    low_lane = lax.broadcasted_iota(jnp.int32, (tiles, LANES), 1) < half
    planes = []
    for seq in range(seqs):
        even = spectra[:tiles, seq * LANES : (seq + 1) * LANES]
        odd = spectra[tiles:, seq * LANES : (seq + 1) * LANES]
        real = jnp.where(low_lane, even, pltpu.roll(odd, half, 1))
        imag = jnp.where(low_lane, pltpu.roll(even, half, 1), odd)
        planes.append((real, imag))
    return planes


WRAP_FROM_ODD = True
WRAP_FROM_EVEN = False
AHEAD_FROM_ODD = False
AHEAD_FROM_EVEN = False


def both(flag, cond):
    return cond if flag else jnp.bool_(False)


def straight(source, d, n_stn):
    wraps = source + d >= n_stn
    odd = lax.rem(source, 2) == 1
    from_odd = both(WRAP_FROM_ODD, wraps) | both(AHEAD_FROM_ODD, ~wraps)
    from_even = both(WRAP_FROM_EVEN, wraps) | both(AHEAD_FROM_EVEN, ~wraps) | (d == 1)
    return (lax.rem(d, 2) == 0) | (odd & from_odd) | (~odd & from_even)


def kernel(
    keeper_ref, x_ref, taps_ref, first_ref, turn_c_ref, turn_s_ref, second_ref, out_ref,
    x_in, taps_in, first_in, turn_c_in, turn_s_in, second_in, keeper_in,
    held, mine, parts, own, others,
    x_sem, taps_sem, const_sem, send_sem, pass_sem, recv_sem,
):
    n_chan, inputs, frames, _, tiles, _ = mine.shape
    n_stn = keeper_ref.shape[0]
    half = parts.shape[0] - 1
    slots = half + 1
    group = n_chan * inputs
    stn = lax.axis_index("stn")
    chan = lax.axis_index("chan")
    odd = lax.rem(stn, 2)
    pair = stn + 1 - 2 * odd
    rows = held.shape[0] // CHUNKS

    loads = []
    for c in range(CHUNKS):
        part = pl.ds(c * rows, rows)
        loads.append((
            pltpu.make_async_copy(x_ref.at[:, :, part], x_in.at[:, :, part], x_sem.at[c]),
            pltpu.make_async_copy(taps_ref.at[:, part], taps_in.at[:, part], taps_sem.at[c]),
        ))
    consts = [
        pltpu.make_async_copy(source, target, const_sem.at[q])
        for q, (source, target) in enumerate([
            (first_ref, first_in), (turn_c_ref, turn_c_in), (turn_s_ref, turn_s_in),
            (second_ref, second_in), (keeper_ref, keeper_in),
        ])
    ]
    for pair_of in loads:
        for load in pair_of:
            load.start()
    for load in consts:
        load.start()

    barrier = pltpu.get_barrier_semaphore()

    def greet(d, carry):
        for step in range(n_chan):
            @pl.when((d > 0) | (step > 0))
            def _():
                there = (lax.rem(stn + n_stn - d, n_stn), lax.rem(chan + step, n_chan))
                pl.semaphore_signal(barrier, inc=1, device_id=there, device_id_type=MESH)
        return carry

    lax.fori_loop(0, half + 1, greet, 0)

    @pl.when(odd == 0)
    def _():
        pl.semaphore_signal(barrier, inc=1, device_id=(pair, chan), device_id_type=MESH)

    for c in range(CHUNKS):
        for load in loads[c]:
            load.wait()
        filter_rows(x_in, taps_in, held, c * rows, rows, inputs, frames)
    for load in consts:
        load.wait()
    planes = transform(held, first_in, turn_c_in, turn_s_in, second_in, inputs * frames)
    for i in range(inputs):
        for f in range(frames):
            for p in range(2):
                plane = planes[i * frames + f][p].astype(jnp.bfloat16)
                for d in range(n_chan):
                    mine[d, i, f, p] = plane[d * tiles : (d + 1) * tiles]
    parts[0, chan] = mine[chan]
    pl.semaphore_wait(barrier, (half + 1) * n_chan - 1 + odd)

    first_wrap = n_stn - stn
    first_far = jnp.where(first_wrap <= half, first_wrap, 1)

    def target(step):
        core = lax.rem(chan, 2)
        return 2 * (step // 2) + lax.rem(core + step, 2)

    def direct(d, step):
        to = target(step)
        return pltpu.make_async_remote_copy(
            src_ref=mine.at[to],
            dst_ref=parts.at[d, chan],
            send_sem=send_sem.at[d, step],
            recv_sem=recv_sem.at[d, chan],
            device_id=(lax.rem(stn + d, n_stn), to),
            device_id_type=MESH,
        )

    def passed(d, origin):
        return pltpu.make_async_remote_copy(
            src_ref=parts.at[d, origin],
            dst_ref=parts.at[d + 1 - 2 * odd, origin],
            send_sem=pass_sem.at[d, origin],
            recv_sem=recv_sem.at[d + 1 - 2 * odd, origin],
            device_id=(pair, chan),
            device_id_type=MESH,
        )

    def passes(d):
        later = d + 1 - 2 * odd
        source = lax.rem(stn + n_stn - d, n_stn)
        return (lax.rem(d, 2) == 0) & (later > 0) & (later < half) & ~straight(source, later, n_stn)

    def far(k):
        return lax.rem(first_far - 1 + k, half) + 1

    def send(k, carry):
        d = far(k)

        @pl.when(straight(stn, d, n_stn))
        def _():
            for step in range(n_chan):
                direct(d, step).start()

        return carry

    lax.fori_loop(0, half, send, 0)
    for step in range(n_chan):
        @pl.when(target(step) != chan)
        def _():
            direct(0, step).start()

    away = lax.rem(stn + half, n_stn)
    row = keeper_in[pl.ds(stn, 1), :]
    column = lax.broadcasted_iota(jnp.int32, row.shape, 1)
    kept = jnp.max(jnp.where(column == away, row, 0), axis=1, keepdims=True)
    kept = jnp.broadcast_to(kept, (group, LANES)) == 1
    base = jnp.where(stn < half, stn + 1, 0)

    def rank(d):
        there = jnp.where(odd == 0, lax.div(half - 1 - d, 2), lax.div(d - 1, 2))
        even = jnp.where(d == 0, 0, 1 + lax.div(half - d, 2))
        return jnp.where(lax.rem(d, 2) == 0, even, half // 2 + 1 + there)

    def at_rank(k):
        odds = k - (half // 2 + 1)
        late = jnp.where(odd == 0, half - 1 - 2 * odds, 1 + 2 * odds)
        even = jnp.where(k == 0, 0, half - 2 * (k - 1))
        return jnp.where(k <= half // 2, even, late)

    def receive(k, carry):
        d = at_rank(k)
        for origin in range(n_chan):
            @pl.when((d > 0) | (origin != chan))
            def _():
                pltpu.make_async_remote_copy(
                    src_ref=mine.at[0],
                    dst_ref=parts.at[d, origin],
                    send_sem=send_sem.at[0, 0],
                    recv_sem=recv_sem.at[d, origin],
                    device_id=(pair, chan),
                    device_id_type=MESH,
                ).wait_recv()

            @pl.when(passes(d))
            def _():
                passed(d, origin).start()

        for f in range(frames):
            for p in range(2):
                value = parts[d, :, :, f, p].astype(jnp.float32).reshape(group, tiles, LANES)
                others[d, f, p] = jnp.transpose(value, (1, 0, 2))

        @pl.when(k == 0)
        def _():
            for f in range(frames):
                for p in range(2):
                    own[f, p] = others[0, f, p] * (1.0 / frames)

        def slot(s, inner):
            single = s < base
            with_far = jnp.where(single, stn - s, half + base - s)
            unfilled = (s == half) & ~single
            without = jnp.where(single | unfilled, with_far, with_far - 1)
            gain = jnp.where(unfilled, 0.0, 1.0).astype(jnp.float32)
            ready = jnp.maximum(rank(with_far), rank(without))

            @pl.when(ready == k)
            def _():
                for t in range(tiles):
                    block = [
                        [jnp.where(kept, others[with_far, f, p, t], others[without, f, p, t] * gain) for p in range(2)]
                        for f in range(frames)
                    ]
                    for i in range(group):
                        real, imag = 0.0, 0.0
                        for f in range(frames):
                            a_re, a_im = [jnp.broadcast_to(own[f, p, t, pl.ds(i, 1), :], (group, LANES)) for p in range(2)]
                            b_re, b_im = block[f]
                            real = real + (a_re * b_re + a_im * b_im)
                            imag = imag + (a_im * b_re - a_re * b_im)
                        lanes = slice(t * LANES, (t + 1) * LANES)
                        out_ref[i, 0, s, :, lanes] = real.astype(jnp.bfloat16)
                        out_ref[i, 1, s, :, lanes] = imag.astype(jnp.bfloat16)

            return inner

        lax.fori_loop(0, slots, slot, 0)
        return carry

    lax.fori_loop(0, half + 1, receive, 0)

    def finish(d, carry):
        @pl.when(straight(stn, d, n_stn))
        def _():
            for step in range(n_chan):
                direct(d, step).wait_send()

        @pl.when(passes(d))
        def _():
            for origin in range(n_chan):
                passed(d, origin).wait_send()

        return carry

    lax.fori_loop(1, half + 1, finish, 0)
    for step in range(n_chan):
        @pl.when(target(step) != chan)
        def _():
            direct(0, step).wait_send()


def per_device(samples, keeper):
    n_stn, n_chan = lax.axis_size("stn"), lax.axis_size("chan")
    inputs, frames_in, _, nfft = samples.shape
    half = n_stn // 2
    frames = frames_in - TAPS + 1
    tiles = CH_WIN // LANES
    n_1 = nfft // LANES
    group = n_chan * inputs
    consts = tables(nfft, CH_WIN * n_chan // n_1)
    x = samples.reshape(inputs, frames_in, 2, n_1, LANES)
    x = jnp.transpose(x, (0, 1, 3, 2, 4)).reshape(inputs, frames_in, 2 * n_1, LANES)
    piece = (n_chan, inputs, frames, 2, tiles, LANES)
    dma = pltpu.SemaphoreType.DMA
    out = pl.pallas_call(
        kernel,
        out_shape=jax.ShapeDtypeStruct((group, 2, half + 1, group, tiles * LANES), jnp.bfloat16),
        in_specs=[pl.BlockSpec(memory_space=pltpu.HBM)] * 7,
        out_specs=pl.BlockSpec(memory_space=pltpu.VMEM),
        scratch_shapes=[
            pltpu.VMEM(x.shape, x.dtype),
            *[pltpu.VMEM(a.shape, jnp.float32) for a in consts],
            pltpu.VMEM(keeper.shape, keeper.dtype),
            pltpu.VMEM((2 * n_1, inputs * frames * LANES), jnp.float32),
            pltpu.VMEM(piece, jnp.bfloat16),
            pltpu.VMEM((half + 1,) + piece, jnp.bfloat16),
            pltpu.VMEM((frames, 2, tiles, group, LANES), jnp.float32),
            pltpu.VMEM((half + 1, frames, 2, tiles, group, LANES), jnp.float32),
            dma((CHUNKS,)),
            dma((CHUNKS,)),
            dma((5,)),
            dma((half + 1, n_chan)),
            dma((half + 1, n_chan)),
            dma((half + 1, n_chan)),
        ],
        compiler_params=pltpu.CompilerParams(collective_id=0, has_side_effects=True, vmem_limit_bytes=VMEM_LIMIT),
        name="correlator",
    )(*[pltpu.with_memory_space_constraint(a, pltpu.HBM) for a in (keeper, x, *[jnp.asarray(c) for c in consts])])
    out = out.reshape(group, 2, (half + 1) * group, tiles * LANES)
    return jnp.transpose(out, (0, 1, 3, 2))


def solution(mesh):
    placed = (P(("stn", "chan"), None, None, None), P())
    return jax.shard_map(
        per_device,
        mesh=mesh,
        in_specs=placed,
        out_specs=P("stn", None, "chan", None),
        check_vma=False,
    )
```

```python
import math

import jax
import jax.numpy as jnp
import numpy as np
from jax import lax
from jax.experimental import pallas as pl
from jax.experimental.pallas import tpu as pltpu
from jax.sharding import PartitionSpec as P

TAPS = 16
LANES = 128
CH_WIN = 1024
MESH = pl.DeviceIdType.MESH
VMEM_LIMIT = 24 << 20
CHUNKS = 4


def tables(nfft, n_k2):
    n_1 = nfft // LANES
    pos = np.arange(TAPS * nfft, dtype=np.float64)
    window = 0.5 - 0.5 * np.cos(2.0 * np.pi * (pos + 0.5) / (TAPS * nfft))
    taps = np.sinc((pos + 0.5) / nfft - TAPS / 2.0) * window
    taps = np.repeat(taps.reshape(TAPS, n_1, LANES), 2, axis=1)
    k_1 = np.arange(n_1)
    n_2 = np.arange(LANES)
    angle = 2.0 * np.pi * (k_1[:, None] * k_1[None, :] % n_1) / n_1
    cosine, sine = np.cos(angle), np.sin(angle)
    first = np.zeros((2, n_1, n_1, 2))
    first[0, :, :, 0] = cosine
    first[0, :, :, 1] = sine
    first[1, :, :, 0] = -sine
    first[1, :, :, 1] = cosine
    first = first.reshape(2 * n_1, 2 * n_1)
    angle = 2.0 * np.pi * (n_2[:, None] * k_1[None, :] % nfft) / nfft
    scale = 1.0 / math.sqrt(nfft)
    turn_c = np.concatenate([np.cos(angle), np.cos(angle)], axis=1) * scale
    turn_s = np.concatenate([np.sin(angle), -np.sin(angle)], axis=1) * scale
    k_2 = np.concatenate([np.arange(0, n_k2, 2), np.arange(1, n_k2, 2)])
    angle = 2.0 * np.pi * (k_2[:, None] * n_2[None, :] % LANES) / LANES
    second = np.concatenate([np.cos(angle), np.sin(angle)], axis=1)
    first = np.concatenate(halves(first), axis=1)
    second = np.concatenate(halves(second), axis=0)
    return [np.asarray(a, np.float32) for a in (taps, turn_c, turn_s)] + [first, second]


def halves(table):
    high = table.astype(jnp.bfloat16)
    return high, (table - high.astype(np.float64)).astype(jnp.bfloat16)


def filter_rows(x_ref, taps_ref, held, first_row, rows, inputs, frames):
    chunk = 16
    for start in range(first_row, first_row + rows, chunk):
        part = slice(start, start + chunk)
        for i in range(inputs):
            totals = [None] * frames
            for step in range(TAPS + frames - 1):
                value = x_ref[i, step, part, :].astype(jnp.float32)
                for f in range(frames):
                    if 0 <= step - f < TAPS:
                        term = value * taps_ref[step - f, part, :]
                        totals[f] = term if totals[f] is None else totals[f] + term
            for f in range(frames):
                seq = i * frames + f
                for q, half in enumerate(split(totals[f])):
                    held[q, part, seq * LANES : (seq + 1) * LANES] = half


def split(value):
    high = value.astype(jnp.bfloat16)
    return high, (value - high.astype(jnp.float32)).astype(jnp.bfloat16)


def dot(a, b):
    return jnp.dot(a, b, preferred_element_type=jnp.float32)


def transform(held, first_ref, turn_c_ref, turn_s_ref, second_ref, seqs):
    half = LANES // 2
    high = held[0]
    depth = high.shape[0]
    stage = dot(first_ref[...], jnp.concatenate([high, high], axis=0)) + dot(first_ref[:, :depth], held[1])
    lane = lax.broadcasted_iota(jnp.int32, (LANES, LANES), 1)
    sign = jnp.where(lane < half, 1.0, -1.0)
    rows = second_ref.shape[0] // 2
    planes = []
    for seq in range(seqs):
        turned = stage[:, seq * LANES : (seq + 1) * LANES].T
        turned = turned * turn_c_ref[...] + pltpu.roll(turned, half, 1) * turn_s_ref[...]
        low = pltpu.roll(turned, half, 1) * sign
        high, rest = split(jnp.concatenate([turned, low], axis=0))
        product = dot(second_ref[...], high)
        spectra = product[:rows] + product[rows:] + dot(second_ref[:rows], rest)
        tiles = rows // 2
        low_lane = lax.broadcasted_iota(jnp.int32, (tiles, LANES), 1) < half
        even, odd = spectra[:tiles], spectra[tiles:]
        real = jnp.where(low_lane, even, pltpu.roll(odd, half, 1))
        imag = jnp.where(low_lane, pltpu.roll(even, half, 1), odd)
        planes.append((real, imag))
    return planes


NEAR_WRAP = False
FAR_WRAP = False
NEAR_AHEAD = False
FAR_AHEAD = False
DOUBLE = False
GATE = 3
LAST = 2


def straight(source, d, n_stn):
    wraps = source + d >= n_stn
    odd = lax.rem(source, 2) == 1
    near = d <= 2
    to_even = (wraps & ((near & NEAR_WRAP) | (~near & FAR_WRAP))) | (~wraps & ((near & NEAR_AHEAD) | (~near & FAR_AHEAD)))
    odd_d = lax.rem(d, 2) == 1
    return (odd & (odd_d == to_even)) | (~odd & (~odd_d | (d == 1))) | (d == 0) | (DOUBLE & odd & wraps & (d == 1))


def kernel(
    keeper_ref, x_ref, taps_ref, turn_c_ref, turn_s_ref, first_ref, second_ref, out_ref,
    x_in, taps_in, turn_c_in, turn_s_in, first_in, second_in, keeper_in,
    held, mine, parts, own, others,
    x_sem, taps_sem, const_sem, send_sem, pass_sem, recv_sem, here_sem,
):
    n_chan, inputs, frames, _, tiles, _ = mine.shape
    n_stn = keeper_ref.shape[0]
    half = parts.shape[0] - 1
    slots = half + 1
    group = n_chan * inputs
    stn = lax.axis_index("stn")
    chan = lax.axis_index("chan")
    odd = lax.rem(stn, 2)
    pair = stn + 1 - 2 * odd
    rows = held.shape[1] // CHUNKS

    loads = []
    for c in range(CHUNKS):
        part = pl.ds(c * rows, rows)
        loads.append((
            pltpu.make_async_copy(x_ref.at[:, :, part], x_in.at[:, :, part], x_sem.at[c]),
            pltpu.make_async_copy(taps_ref.at[:, part], taps_in.at[:, part], taps_sem.at[c]),
        ))
    consts = [
        pltpu.make_async_copy(source, target, const_sem.at[q])
        for q, (source, target) in enumerate([
            (first_ref, first_in), (turn_c_ref, turn_c_in), (turn_s_ref, turn_s_in),
            (second_ref, second_in), (keeper_ref, keeper_in),
        ])
    ]
    for pair_of in loads:
        for load in pair_of:
            load.start()
    for load in consts:
        load.start()

    barrier = pltpu.get_barrier_semaphore()

    def signal_all(semaphore, there):
        for step in range(n_chan):
            to = lax.rem(chan + step, n_chan)
            pl.semaphore_signal(semaphore, inc=1, device_id=(there, to), device_id_type=MESH)

    def enter(d, carry):
        @pl.when(d > stn)
        def _():
            signal_all(barrier, stn - d + n_stn)

        @pl.when(stn + d < n_stn)
        def _():
            signal_all(barrier, stn + d)

        return carry

    lax.fori_loop(1, half + 1, enter, 0)
    for step in range(1, n_chan):
        there = (stn, lax.rem(chan + step, n_chan))
        pl.semaphore_signal(barrier, inc=1, device_id=there, device_id_type=MESH)

    for c in range(CHUNKS):
        for load in loads[c]:
            load.wait()
        filter_rows(x_in, taps_in, held, c * rows, rows, inputs, frames)
    back = jnp.maximum(stn - half + 1, 0)
    pl.semaphore_wait(barrier, (back + jnp.minimum(stn, half) + 1) * n_chan - 1)

    def answer(d, carry):
        @pl.when(d <= stn)
        def _():
            signal_all(here_sem.at[d], stn - d)

        return carry

    lax.fori_loop(1, half + 1, answer, 0)
    for load in consts:
        load.wait()
    planes = transform(held, first_in, turn_c_in, turn_s_in, second_in, inputs * frames)
    for i in range(inputs):
        for f in range(frames):
            for p in range(2):
                plane = planes[i * frames + f][p].astype(jnp.bfloat16)
                for d in range(n_chan):
                    mine[d, i, f, p] = plane[d * tiles : (d + 1) * tiles]
    parts[0, chan] = mine[chan]

    def target(step):
        core = lax.rem(chan, 2)
        return 2 * (step // 2) + lax.rem(core + step, 2)

    def direct(d, step):
        to = target(step)
        return pltpu.make_async_remote_copy(
            src_ref=mine.at[to],
            dst_ref=parts.at[d, chan],
            send_sem=send_sem.at[d, step],
            recv_sem=recv_sem.at[d, chan],
            device_id=(lax.rem(stn + d, n_stn), to),
            device_id_type=MESH,
        )

    def passed(d, origin):
        return pltpu.make_async_remote_copy(
            src_ref=parts.at[d, origin],
            dst_ref=parts.at[d + 1 - 2 * odd, origin],
            send_sem=pass_sem.at[d, origin],
            recv_sem=recv_sem.at[d + 1 - 2 * odd, origin],
            device_id=(pair, chan),
            device_id_type=MESH,
        )

    def passes(d):
        later = d + 1 - 2 * odd
        source = lax.rem(stn + n_stn - d, n_stn)
        needed = (d > 0) & (later > 0) & (later <= half)
        return needed & straight(source, d, n_stn) & ~straight(source, later, n_stn)

    def late(d):
        return stn + d >= n_stn + LAST

    def send(d, carry):
        @pl.when((stn + d >= n_stn) & ~late(d) & straight(stn, d, n_stn))
        def _():
            for step in range(n_chan):
                direct(d, step).start()

        return carry

    def gates(d):
        return (stn + half >= n_stn + LAST) & (stn + d >= n_stn) & ~late(d) & straight(stn, d, n_stn)

    def gate(d, carry):
        @pl.when(gates(d))
        def _():
            direct(d, GATE).wait_send()

        return carry

    def send_late(d, carry):
        @pl.when(late(d) & straight(stn, d, n_stn))
        def _():
            for step in range(n_chan):
                direct(d, step).start()

        return carry

    def send_ahead(d, carry):
        @pl.when(stn + d < n_stn)
        def _():
            pl.semaphore_wait(here_sem.at[d], n_chan)

            @pl.when(straight(stn, d, n_stn))
            def _():
                for step in range(n_chan):
                    direct(d, step).start()

        return carry

    for step in range(n_chan):
        @pl.when(target(step) != chan)
        def _():
            direct(0, step).start()
    lax.fori_loop(1, half + 1, send, 0)
    lax.fori_loop(1, half + 1, send_ahead, 0)
    lax.fori_loop(1, half + 1, gate, 0)
    lax.fori_loop(1, half + 1, send_late, 0)

    away = lax.rem(stn + half, n_stn)
    row = keeper_in[pl.ds(stn, 1), :]
    column = lax.broadcasted_iota(jnp.int32, row.shape, 1)
    kept = jnp.max(jnp.where(column == away, row, 0), axis=1, keepdims=True)
    kept = jnp.broadcast_to(kept, (group, LANES)) == 1
    base = jnp.where(stn < half, stn + 1, 0)

    ahead = jnp.minimum(stn, half)

    def comes_straight(d):
        return straight(lax.rem(stn + n_stn - d, n_stn), d, n_stn)

    def rank(d):
        place = jnp.where(d <= ahead, d, half + 1 + ahead - d)
        return jnp.where(comes_straight(d), place, place + slots)

    def at_rank(k):
        return jnp.where(k <= ahead, k, half + 1 + ahead - k)

    def receive(k, carry):
        d = at_rank(lax.rem(k, slots))

        @pl.when(comes_straight(d) == (k < slots))
        def _():
            take(k, d)

        return carry

    def take(k, d):
        for origin in range(n_chan):
            @pl.when((d > 0) | (origin != chan))
            def _():
                pltpu.make_async_remote_copy(
                    src_ref=mine.at[0],
                    dst_ref=parts.at[d, origin],
                    send_sem=send_sem.at[0, 0],
                    recv_sem=recv_sem.at[d, origin],
                    device_id=(pair, chan),
                    device_id_type=MESH,
                ).wait_recv()

            @pl.when(passes(d))
            def _():
                passed(d, origin).start()

        for f in range(frames):
            for p in range(2):
                value = parts[d, :, :, f, p].astype(jnp.float32).reshape(group, tiles, LANES)
                others[d, f, p] = jnp.transpose(value, (1, 0, 2))

        @pl.when(k == 0)
        def _():
            for f in range(frames):
                for p in range(2):
                    own[f, p] = others[0, f, p] * (1.0 / frames)

        def slot(s, inner):
            single = s < base
            with_far = jnp.where(single, stn - s, half + base - s)
            unfilled = (s == half) & ~single
            without = jnp.where(single | unfilled, with_far, with_far - 1)
            gain = jnp.where(unfilled, 0.0, 1.0).astype(jnp.float32)
            ready = jnp.maximum(rank(with_far), rank(without))

            @pl.when(ready == k)
            def _():
                for t in range(tiles):
                    block = [
                        [jnp.where(kept, others[with_far, f, p, t], others[without, f, p, t] * gain) for p in range(2)]
                        for f in range(frames)
                    ]
                    for i in range(group):
                        real, imag = 0.0, 0.0
                        for f in range(frames):
                            a_re, a_im = [jnp.broadcast_to(own[f, p, t, pl.ds(i, 1), :], (group, LANES)) for p in range(2)]
                            b_re, b_im = block[f]
                            real = real + (a_re * b_re + a_im * b_im)
                            imag = imag + (a_im * b_re - a_re * b_im)
                        lanes = slice(t * LANES, (t + 1) * LANES)
                        out_ref[i, 0, s, :, lanes] = real.astype(jnp.bfloat16)
                        out_ref[i, 1, s, :, lanes] = imag.astype(jnp.bfloat16)

            return inner

        lax.fori_loop(0, slots, slot, 0)

    lax.fori_loop(0, 2 * slots, receive, 0)

    def finish(d, carry):
        @pl.when(straight(stn, d, n_stn))
        def _():
            for step in range(n_chan):
                if step != GATE:
                    direct(d, step).wait_send()

        @pl.when(straight(stn, d, n_stn) & ~gates(d))
        def _():
            direct(d, GATE).wait_send()

        @pl.when(passes(d))
        def _():
            for origin in range(n_chan):
                passed(d, origin).wait_send()

        return carry

    lax.fori_loop(1, half + 1, finish, 0)
    for step in range(n_chan):
        @pl.when(target(step) != chan)
        def _():
            direct(0, step).wait_send()


def per_device(samples, keeper):
    n_stn, n_chan = lax.axis_size("stn"), lax.axis_size("chan")
    inputs, frames_in, _, nfft = samples.shape
    half = n_stn // 2
    frames = frames_in - TAPS + 1
    tiles = CH_WIN // LANES
    n_1 = nfft // LANES
    group = n_chan * inputs
    consts = tables(nfft, CH_WIN * n_chan // n_1)
    x = samples.reshape(inputs, frames_in, 2, n_1, LANES)
    x = jnp.transpose(x, (0, 1, 3, 2, 4)).reshape(inputs, frames_in, 2 * n_1, LANES)
    piece = (n_chan, inputs, frames, 2, tiles, LANES)
    dma = pltpu.SemaphoreType.DMA
    out = pl.pallas_call(
        kernel,
        out_shape=jax.ShapeDtypeStruct((group, 2, half + 1, group, tiles * LANES), jnp.bfloat16),
        in_specs=[pl.BlockSpec(memory_space=pltpu.HBM)] * 7,
        out_specs=pl.BlockSpec(memory_space=pltpu.VMEM),
        scratch_shapes=[
            pltpu.VMEM(x.shape, x.dtype),
            *[pltpu.VMEM(a.shape, a.dtype) for a in consts],
            pltpu.VMEM(keeper.shape, keeper.dtype),
            pltpu.VMEM((2, 2 * n_1, inputs * frames * LANES), jnp.bfloat16),
            pltpu.VMEM(piece, jnp.bfloat16),
            pltpu.VMEM((half + 1,) + piece, jnp.bfloat16),
            pltpu.VMEM((frames, 2, tiles, group, LANES), jnp.float32),
            pltpu.VMEM((half + 1, frames, 2, tiles, group, LANES), jnp.float32),
            dma((CHUNKS,)),
            dma((CHUNKS,)),
            dma((5,)),
            dma((half + 1, n_chan)),
            dma((half + 1, n_chan)),
            dma((half + 1, n_chan)),
            pltpu.SemaphoreType.REGULAR((half + 1,)),
        ],
        compiler_params=pltpu.CompilerParams(collective_id=0, has_side_effects=True, vmem_limit_bytes=VMEM_LIMIT),
        name="correlator",
    )(*[pltpu.with_memory_space_constraint(a, pltpu.HBM) for a in (keeper, x, *[jnp.asarray(c) for c in consts])])
    out = out.reshape(group, 2, (half + 1) * group, tiles * LANES)
    return jnp.transpose(out, (0, 1, 3, 2))


def solution(mesh):
    placed = (P(("stn", "chan"), None, None, None), P())
    return jax.shard_map(
        per_device,
        mesh=mesh,
        in_specs=placed,
        out_specs=P("stn", None, "chan", None),
        check_vma=False,
    )
```

```python
import math

import jax
import jax.numpy as jnp
import numpy as np
from jax import lax
from jax.experimental import pallas as pl
from jax.experimental.pallas import tpu as pltpu
from jax.sharding import PartitionSpec as P

TAPS = 16
LANES = 128
CH_WIN = 1024
MESH = pl.DeviceIdType.MESH
VMEM_LIMIT = 24 << 20
CHUNKS = 4


def tables(nfft, n_k2):
    n_1 = nfft // LANES
    pos = np.arange(TAPS * nfft, dtype=np.float64)
    window = 0.5 - 0.5 * np.cos(2.0 * np.pi * (pos + 0.5) / (TAPS * nfft))
    taps = np.sinc((pos + 0.5) / nfft - TAPS / 2.0) * window
    taps = np.repeat(taps.reshape(TAPS, n_1, LANES), 2, axis=1)
    k_1 = np.arange(n_1)
    n_2 = np.arange(LANES)
    angle = 2.0 * np.pi * (k_1[:, None] * k_1[None, :] % n_1) / n_1
    cosine, sine = np.cos(angle), np.sin(angle)
    first = np.zeros((2, n_1, n_1, 2))
    first[0, :, :, 0] = cosine
    first[0, :, :, 1] = sine
    first[1, :, :, 0] = -sine
    first[1, :, :, 1] = cosine
    first = first.reshape(2 * n_1, 2 * n_1)
    angle = 2.0 * np.pi * (n_2[:, None] * k_1[None, :] % nfft) / nfft
    scale = 1.0 / math.sqrt(nfft)
    turn_c = np.concatenate([np.cos(angle), np.cos(angle)], axis=1) * scale
    turn_s = np.concatenate([np.sin(angle), -np.sin(angle)], axis=1) * scale
    k_2 = np.concatenate([np.arange(0, n_k2, 2), np.arange(1, n_k2, 2)])
    angle = 2.0 * np.pi * (k_2[:, None] * n_2[None, :] % LANES) / LANES
    second = np.concatenate([np.cos(angle), np.sin(angle)], axis=1)
    first = np.concatenate(halves(first), axis=1)
    second = np.concatenate(halves(second), axis=0)
    return [np.asarray(a, np.float32) for a in (taps, turn_c, turn_s)] + [first, second]


def halves(table):
    high = table.astype(jnp.bfloat16)
    return high, (table - high.astype(np.float64)).astype(jnp.bfloat16)


def filter_rows(x_ref, taps_ref, held, first_row, rows, inputs, frames):
    chunk = 16
    for start in range(first_row, first_row + rows, chunk):
        part = slice(start, start + chunk)
        for i in range(inputs):
            totals = [None] * frames
            for step in range(TAPS + frames - 1):
                value = x_ref[i, step, part, :].astype(jnp.float32)
                for f in range(frames):
                    if 0 <= step - f < TAPS:
                        term = value * taps_ref[step - f, part, :]
                        totals[f] = term if totals[f] is None else totals[f] + term
            for f in range(frames):
                seq = i * frames + f
                for q, half in enumerate(split(totals[f])):
                    held[q, part, seq * LANES : (seq + 1) * LANES] = half


def split(value):
    high = value.astype(jnp.bfloat16)
    return high, (value - high.astype(jnp.float32)).astype(jnp.bfloat16)


def dot(a, b):
    return jnp.dot(a, b, preferred_element_type=jnp.float32)


def transform(held, first_ref, turn_c_ref, turn_s_ref, second_ref, seqs):
    half = LANES // 2
    high = held[0]
    depth = high.shape[0]
    stage = dot(first_ref[...], jnp.concatenate([high, high], axis=0)) + dot(first_ref[:, :depth], held[1])
    lane = lax.broadcasted_iota(jnp.int32, (LANES, LANES), 1)
    sign = jnp.where(lane < half, 1.0, -1.0)
    rows = second_ref.shape[0] // 2
    planes = []
    his = []
    for seq in range(seqs):
        turned = stage[:, seq * LANES : (seq + 1) * LANES].T
        turned = turned * turn_c_ref[...] + pltpu.roll(turned, half, 1) * turn_s_ref[...]
        low = pltpu.roll(turned, half, 1) * sign
        his.append(jnp.concatenate([turned, low], axis=0))
    high, rest = split(jnp.concatenate(his, axis=1))
    product = dot(second_ref[...], high)
    every = product[:rows] + product[rows:] + dot(second_ref[:rows], rest)
    for seq in range(seqs):
        spectra = every[:, seq * LANES : (seq + 1) * LANES]
        tiles = rows // 2
        low_lane = lax.broadcasted_iota(jnp.int32, (tiles, LANES), 1) < half
        even, odd = spectra[:tiles], spectra[tiles:]
        real = jnp.where(low_lane, even, pltpu.roll(odd, half, 1))
        imag = jnp.where(low_lane, pltpu.roll(even, half, 1), odd)
        planes.append((real, imag))
    return planes


GATE = 3
LAST = 2


def straight(source, origin, d, n_stn):
    odd = lax.rem(source, 2) == 1
    odd_d = lax.rem(d, 2) == 1
    to_even = (source + d >= n_stn) & (d > 2) & (lax.rem(origin, 2) == 0)
    return (odd & (odd_d == to_even)) | (~odd & (~odd_d | (d == 1))) | (d == 0)


def kernel(
    keeper_ref, x_ref, taps_ref, turn_c_ref, turn_s_ref, first_ref, second_ref, out_ref,
    x_in, taps_in, turn_c_in, turn_s_in, first_in, second_in, keeper_in,
    held, mine, parts, own, others,
    x_sem, taps_sem, const_sem, send_sem, pass_sem, recv_sem, here_sem,
):
    n_chan, inputs, frames, _, tiles, _ = mine.shape
    n_stn = keeper_ref.shape[0]
    half = parts.shape[0] - 1
    slots = half + 1
    group = n_chan * inputs
    stn = lax.axis_index("stn")
    chan = lax.axis_index("chan")
    odd = lax.rem(stn, 2)
    pair = stn + 1 - 2 * odd
    rows = held.shape[1] // CHUNKS

    loads = []
    for c in range(CHUNKS):
        part = pl.ds(c * rows, rows)
        loads.append((
            pltpu.make_async_copy(x_ref.at[:, :, part], x_in.at[:, :, part], x_sem.at[c]),
            pltpu.make_async_copy(taps_ref.at[:, part], taps_in.at[:, part], taps_sem.at[c]),
        ))
    consts = [
        pltpu.make_async_copy(source, target, const_sem.at[q])
        for q, (source, target) in enumerate([
            (first_ref, first_in), (turn_c_ref, turn_c_in), (turn_s_ref, turn_s_in),
            (second_ref, second_in), (keeper_ref, keeper_in),
        ])
    ]
    for pair_of in loads:
        for load in pair_of:
            load.start()
    for load in consts:
        load.start()

    barrier = pltpu.get_barrier_semaphore()

    def signal_all(semaphore, there):
        for step in range(n_chan):
            to = lax.rem(chan + step, n_chan)
            pl.semaphore_signal(semaphore, inc=1, device_id=(there, to), device_id_type=MESH)

    def enter(d, carry):
        @pl.when(d > stn)
        def _():
            signal_all(barrier, stn - d + n_stn)

        @pl.when(stn + d < n_stn)
        def _():
            signal_all(barrier, stn + d)

        return carry

    lax.fori_loop(1, half + 1, enter, 0)
    for step in range(1, n_chan):
        there = (stn, lax.rem(chan + step, n_chan))
        pl.semaphore_signal(barrier, inc=1, device_id=there, device_id_type=MESH)

    for c in range(CHUNKS):
        for load in loads[c]:
            load.wait()
        filter_rows(x_in, taps_in, held, c * rows, rows, inputs, frames)
    for load in consts:
        load.wait()
    planes = transform(held, first_in, turn_c_in, turn_s_in, second_in, inputs * frames)
    for i in range(inputs):
        for f in range(frames):
            for p in range(2):
                plane = planes[i * frames + f][p].astype(jnp.bfloat16)
                for d in range(n_chan):
                    mine[d, i, f, p] = plane[d * tiles : (d + 1) * tiles]
    parts[0, chan] = mine[chan]

    def target(step):
        core = lax.rem(chan, 2)
        return 2 * (step // 2) + lax.rem(core + step, 2)

    def direct(d, step):
        to = target(step)
        return pltpu.make_async_remote_copy(
            src_ref=mine.at[to],
            dst_ref=parts.at[d, chan],
            send_sem=send_sem.at[d, step],
            recv_sem=recv_sem.at[d, chan],
            device_id=(lax.rem(stn + d, n_stn), to),
            device_id_type=MESH,
        )

    def passed(d, origin):
        return pltpu.make_async_remote_copy(
            src_ref=parts.at[d, origin],
            dst_ref=parts.at[d + 1 - 2 * odd, origin],
            send_sem=pass_sem.at[d, origin],
            recv_sem=recv_sem.at[d + 1 - 2 * odd, origin],
            device_id=(pair, chan),
            device_id_type=MESH,
        )

    def passes(d, origin):
        later = d + 1 - 2 * odd
        source = lax.rem(stn + n_stn - d, n_stn)
        needed = (d > 0) & (later > 0) & (later <= half)
        return needed & straight(source, origin, d, n_stn) & ~straight(source, origin, later, n_stn)

    def late(d):
        return stn + d >= n_stn + LAST

    def send(d, carry):
        @pl.when((stn + d >= n_stn) & ~late(d) & straight(stn, chan, d, n_stn))
        def _():
            for step in range(n_chan):
                direct(d, step).start()

        return carry

    def gates(d):
        return (stn + half >= n_stn + LAST) & (stn + d >= n_stn) & ~late(d) & straight(stn, chan, d, n_stn)

    def gate(d, carry):
        @pl.when(gates(d))
        def _():
            direct(d, GATE).wait_send()

        return carry

    def send_late(d, carry):
        @pl.when(late(d) & straight(stn, chan, d, n_stn))
        def _():
            for step in range(n_chan):
                direct(d, step).start()

        return carry

    def send_ahead(d, carry):
        @pl.when(stn + d < n_stn)
        def _():
            pl.semaphore_wait(here_sem.at[d], 1)

            @pl.when(straight(stn, chan, d, n_stn))
            def _():
                for step in range(n_chan):
                    direct(d, step).start()

        return carry

    back = jnp.maximum(stn - half + 1, 0)
    pl.semaphore_wait(barrier, (back + jnp.minimum(stn, half) + 1) * n_chan - 1)


    def answer(d, carry):
        @pl.when(d <= stn)
        def _():
            pl.semaphore_signal(here_sem.at[d], inc=1, device_id=(stn - d, chan), device_id_type=MESH)

        return carry

    lax.fori_loop(1, half + 1, answer, 0)
    last = stn + half >= n_stn + LAST

    @pl.when(~last)
    def _():
        lax.fori_loop(1, half + 1, send, 0)

    for step in range(n_chan):
        @pl.when(target(step) != chan)
        def _():
            direct(0, step).start()

    @pl.when(last)
    def _():
        lax.fori_loop(1, half + 1, send, 0)

    lax.fori_loop(1, half + 1, send_ahead, 0)
    lax.fori_loop(1, half + 1, gate, 0)
    lax.fori_loop(1, half + 1, send_late, 0)

    away = lax.rem(stn + half, n_stn)
    row = keeper_in[pl.ds(stn, 1), :]
    column = lax.broadcasted_iota(jnp.int32, row.shape, 1)
    kept = jnp.max(jnp.where(column == away, row, 0), axis=1, keepdims=True)
    kept = jnp.broadcast_to(kept, (group, LANES)) == 1
    base = jnp.where(stn < half, stn + 1, 0)

    ahead = jnp.minimum(stn, half)

    def comes_straight(d, origin):
        return straight(lax.rem(stn + n_stn - d, n_stn), origin, d, n_stn)

    def all_straight(d):
        every = comes_straight(d, 0)
        for origin in range(1, n_chan):
            every = every & comes_straight(d, origin)
        return every

    def rank(d):
        place = jnp.where(d <= ahead, d, half + 1 + ahead - d)
        return jnp.where(all_straight(d), place, place + slots)

    def at_rank(k):
        return jnp.where(k <= ahead, k, half + 1 + ahead - k)

    def receive(k, carry):
        d = at_rank(lax.rem(k, slots))
        for origin in range(n_chan):
            here = (d == 0) & (origin == chan)

            @pl.when((comes_straight(d, origin) == (k < slots)) & ~here)
            def _():
                pltpu.make_async_remote_copy(
                    src_ref=mine.at[0],
                    dst_ref=parts.at[d, origin],
                    send_sem=send_sem.at[0, 0],
                    recv_sem=recv_sem.at[d, origin],
                    device_id=(pair, chan),
                    device_id_type=MESH,
                ).wait_recv()

            @pl.when((k < slots) & passes(d, origin))
            def _():
                passed(d, origin).start()

        @pl.when(all_straight(d) == (k < slots))
        def _():
            take(k, d)

        return carry

    def take(k, d):
        for f in range(frames):
            for p in range(2):
                value = parts[d, :, :, f, p].astype(jnp.float32).reshape(group, tiles, LANES)
                others[d, f, p] = jnp.transpose(value, (1, 0, 2))

        @pl.when(k == 0)
        def _():
            for f in range(frames):
                for p in range(2):
                    own[f, p] = others[0, f, p] * (1.0 / frames)

        def slot(s, inner):
            single = s < base
            with_far = jnp.where(single, stn - s, half + base - s)
            unfilled = (s == half) & ~single
            without = jnp.where(single | unfilled, with_far, with_far - 1)
            gain = jnp.where(unfilled, 0.0, 1.0).astype(jnp.float32)
            ready = jnp.maximum(rank(with_far), rank(without))

            @pl.when(ready == k)
            def _():
                for t in range(tiles):
                    block = [
                        [jnp.where(kept, others[with_far, f, p, t], others[without, f, p, t] * gain) for p in range(2)]
                        for f in range(frames)
                    ]
                    for i in range(group):
                        real, imag = 0.0, 0.0
                        for f in range(frames):
                            a_re, a_im = [jnp.broadcast_to(own[f, p, t, pl.ds(i, 1), :], (group, LANES)) for p in range(2)]
                            b_re, b_im = block[f]
                            real = real + (a_re * b_re + a_im * b_im)
                            imag = imag + (a_im * b_re - a_re * b_im)
                        lanes = slice(t * LANES, (t + 1) * LANES)
                        out_ref[i, 0, s, :, lanes] = real.astype(jnp.bfloat16)
                        out_ref[i, 1, s, :, lanes] = imag.astype(jnp.bfloat16)

            return inner

        lax.fori_loop(0, slots, slot, 0)

    lax.fori_loop(0, 2 * slots, receive, 0)

    def finish(d, carry):
        @pl.when(straight(stn, chan, d, n_stn))
        def _():
            for step in range(n_chan):
                if step != GATE:
                    direct(d, step).wait_send()

        @pl.when(straight(stn, chan, d, n_stn) & ~gates(d))
        def _():
            direct(d, GATE).wait_send()

        for origin in range(n_chan):
            @pl.when(passes(d, origin))
            def _():
                passed(d, origin).wait_send()

        return carry

    lax.fori_loop(1, half + 1, finish, 0)
    for step in range(n_chan):
        @pl.when(target(step) != chan)
        def _():
            direct(0, step).wait_send()


def per_device(samples, keeper):
    n_stn, n_chan = lax.axis_size("stn"), lax.axis_size("chan")
    inputs, frames_in, _, nfft = samples.shape
    half = n_stn // 2
    frames = frames_in - TAPS + 1
    tiles = CH_WIN // LANES
    n_1 = nfft // LANES
    group = n_chan * inputs
    consts = tables(nfft, CH_WIN * n_chan // n_1)
    x = samples.reshape(inputs, frames_in, 2, n_1, LANES)
    x = jnp.transpose(x, (0, 1, 3, 2, 4)).reshape(inputs, frames_in, 2 * n_1, LANES)
    piece = (n_chan, inputs, frames, 2, tiles, LANES)
    dma = pltpu.SemaphoreType.DMA
    out = pl.pallas_call(
        kernel,
        out_shape=jax.ShapeDtypeStruct((group, 2, half + 1, group, tiles * LANES), jnp.bfloat16),
        in_specs=[pl.BlockSpec(memory_space=pltpu.HBM)] * 7,
        out_specs=pl.BlockSpec(memory_space=pltpu.VMEM),
        scratch_shapes=[
            pltpu.VMEM(x.shape, x.dtype),
            *[pltpu.VMEM(a.shape, a.dtype) for a in consts],
            pltpu.VMEM(keeper.shape, keeper.dtype),
            pltpu.VMEM((2, 2 * n_1, inputs * frames * LANES), jnp.bfloat16),
            pltpu.VMEM(piece, jnp.bfloat16),
            pltpu.VMEM((half + 1,) + piece, jnp.bfloat16),
            pltpu.VMEM((frames, 2, tiles, group, LANES), jnp.float32),
            pltpu.VMEM((half + 1, frames, 2, tiles, group, LANES), jnp.float32),
            dma((CHUNKS,)),
            dma((CHUNKS,)),
            dma((5,)),
            dma((half + 1, n_chan)),
            dma((half + 1, n_chan)),
            dma((half + 1, n_chan)),
            pltpu.SemaphoreType.REGULAR((half + 1,)),
        ],
        compiler_params=pltpu.CompilerParams(collective_id=0, has_side_effects=True, vmem_limit_bytes=VMEM_LIMIT),
        name="correlator",
    )(*[pltpu.with_memory_space_constraint(a, pltpu.HBM) for a in (keeper, x, *[jnp.asarray(c) for c in consts])])
    out = out.reshape(group, 2, (half + 1) * group, tiles * LANES)
    return jnp.transpose(out, (0, 1, 3, 2))


def solution(mesh):
    placed = (P(("stn", "chan"), None, None, None), P())
    return jax.shard_map(
        per_device,
        mesh=mesh,
        in_specs=placed,
        out_specs=P("stn", None, "chan", None),
        check_vma=False,
    )
```

```python
import math

import jax
import jax.numpy as jnp
import numpy as np
from jax import lax
from jax.experimental import pallas as pl
from jax.experimental.pallas import tpu as pltpu
from jax.sharding import PartitionSpec as P

TAPS = 16
LANES = 128
CH_WIN = 1024
MESH = pl.DeviceIdType.MESH
VMEM_LIMIT = 24 << 20
CHUNKS = 4


def tables(nfft, n_k2):
    n_1 = nfft // LANES
    k_1 = np.arange(n_1)
    n_2 = np.arange(LANES)
    angle = 2.0 * np.pi * (k_1[:, None] * k_1[None, :] % n_1) / n_1
    cosine, sine = np.cos(angle), np.sin(angle)
    first = np.zeros((2, n_1, n_1, 2))
    first[0, :, :, 0] = cosine
    first[0, :, :, 1] = sine
    first[1, :, :, 0] = -sine
    first[1, :, :, 1] = cosine
    first = first.reshape(2 * n_1, 2 * n_1)
    angle = 2.0 * np.pi * (n_2[:, None] * k_1[None, :] % nfft) / nfft
    scale = 1.0 / math.sqrt(nfft)
    turn_c = np.concatenate([np.cos(angle), np.cos(angle)], axis=1) * scale
    turn_s = np.concatenate([np.sin(angle), -np.sin(angle)], axis=1) * scale
    k_2 = np.concatenate([np.arange(0, n_k2, 2), np.arange(1, n_k2, 2)])
    angle = 2.0 * np.pi * (k_2[:, None] * n_2[None, :] % LANES) / LANES
    second = np.concatenate([np.cos(angle), np.sin(angle)], axis=1)
    first = np.concatenate(halves(first), axis=1)
    second = np.concatenate(halves(second), axis=0)
    return [np.asarray(a, np.float32) for a in (turn_c, turn_s)] + [first, second]


def halves(table):
    high = table.astype(jnp.bfloat16)
    return high, (table - high.astype(np.float64)).astype(jnp.bfloat16)


def series(square, terms):
    total = jnp.full_like(square, terms[-1])
    for term in reversed(terms[:-1]):
        total = total * square + term
    return total


def make_taps(taps_ref):
    rows = taps_ref.shape[1]
    nfft = rows // 2 * LANES
    height = 8
    odd = [(-1) ** q * math.pi ** (2 * q) / math.factorial(2 * q + 1) for q in range(7)]
    turn = 2.0 * math.pi / TAPS
    cosine = [(-1) ** q * turn ** (2 * q) / math.factorial(2 * q) for q in range(5)]
    sine = [(-1) ** q * turn ** (2 * q + 1) / math.factorial(2 * q + 1) for q in range(5)]

    def block(j, carry):
        start = pl.multiple_of(j * height, height)
        row = lax.broadcasted_iota(jnp.int32, (height, LANES), 0) + start
        lane = lax.broadcasted_iota(jnp.int32, (height, LANES), 1)
        u = (lax.div(row, 2) * LANES + lane).astype(jnp.float32) * (1.0 / nfft) + 0.5 / nfft
        near = jnp.minimum(u, 1.0 - u)
        wave = near * series(near * near, odd)
        square = u * u
        cos_u, sin_u = series(square, cosine), u * series(square, sine)
        for t in range(TAPS):
            sign = -1.0 if t % 2 else 1.0
            c, s = math.cos(turn * t) * 0.5 * sign, math.sin(turn * t) * 0.5 * sign
            window = (0.5 * sign - c * cos_u) + s * sin_u
            taps_ref[t, pl.ds(start, height), :] = wave * window / (u + (t - TAPS // 2))
        return carry

    lax.fori_loop(0, rows // height, block, 0)


def filter_rows(x_ref, taps_ref, held, first_row, rows, inputs, frames):
    chunk = 16
    for start in range(first_row, first_row + rows, chunk):
        part = slice(start, start + chunk)
        for i in range(inputs):
            totals = [None] * frames
            for step in range(TAPS + frames - 1):
                value = x_ref[i, step, part, :].astype(jnp.float32)
                for f in range(frames):
                    if 0 <= step - f < TAPS:
                        term = value * taps_ref[step - f, part, :]
                        totals[f] = term if totals[f] is None else totals[f] + term
            for f in range(frames):
                seq = i * frames + f
                for q, half in enumerate(split(totals[f])):
                    held[q, part, seq * LANES : (seq + 1) * LANES] = half


def split(value):
    high = value.astype(jnp.bfloat16)
    return high, (value - high.astype(jnp.float32)).astype(jnp.bfloat16)


def dot(a, b):
    return jnp.dot(a, b, preferred_element_type=jnp.float32)


def transform(held, first_ref, turn_c_ref, turn_s_ref, second_ref, seqs):
    half = LANES // 2
    high = held[0]
    depth = high.shape[0]
    stage = dot(first_ref[...], jnp.concatenate([high, high], axis=0)) + dot(first_ref[:, :depth], held[1])
    lane = lax.broadcasted_iota(jnp.int32, (LANES, LANES), 1)
    sign = jnp.where(lane < half, 1.0, -1.0)
    rows = second_ref.shape[0] // 2
    planes = []
    his = []
    for seq in range(seqs):
        turned = stage[:, seq * LANES : (seq + 1) * LANES].T
        turned = turned * turn_c_ref[...] + pltpu.roll(turned, half, 1) * turn_s_ref[...]
        low = pltpu.roll(turned, half, 1) * sign
        his.append(jnp.concatenate([turned, low], axis=0))
    high, rest = split(jnp.concatenate(his, axis=1))
    product = dot(second_ref[...], high)
    every = product[:rows] + product[rows:] + dot(second_ref[:rows], rest)
    for seq in range(seqs):
        spectra = every[:, seq * LANES : (seq + 1) * LANES]
        tiles = rows // 2
        low_lane = lax.broadcasted_iota(jnp.int32, (tiles, LANES), 1) < half
        even, odd = spectra[:tiles], spectra[tiles:]
        real = jnp.where(low_lane, even, pltpu.roll(odd, half, 1))
        imag = jnp.where(low_lane, pltpu.roll(even, half, 1), odd)
        planes.append((real, imag))
    return planes


GATE = 3
LAST = 2


def straight(source, origin, d, n_stn):
    odd = lax.rem(source, 2) == 1
    odd_d = lax.rem(d, 2) == 1
    to_even = (source + d >= n_stn) & (d > 2) & (lax.rem(origin, 2) == 0)
    return (odd & (odd_d == to_even)) | (~odd & (~odd_d | (d == 1))) | (d == 0)


def kernel(
    keeper_ref, x_ref, turn_c_ref, turn_s_ref, first_ref, second_ref, out_ref,
    x_in, taps_in, turn_c_in, turn_s_in, first_in, second_in, keeper_in,
    held, mine, parts, own, others,
    x_sem, const_sem, send_sem, pass_sem, recv_sem, here_sem,
):
    n_chan, inputs, frames, _, tiles, _ = mine.shape
    n_stn = keeper_ref.shape[0]
    half = parts.shape[0] - 1
    slots = half + 1
    group = n_chan * inputs
    stn = lax.axis_index("stn")
    chan = lax.axis_index("chan")
    odd = lax.rem(stn, 2)
    pair = stn + 1 - 2 * odd
    rows = held.shape[1] // CHUNKS

    loads = []
    for c in range(CHUNKS):
        part = pl.ds(c * rows, rows)
        loads.append(pltpu.make_async_copy(x_ref.at[:, :, part], x_in.at[:, :, part], x_sem.at[c]))
    consts = [
        pltpu.make_async_copy(source, target, const_sem.at[q])
        for q, (source, target) in enumerate([
            (first_ref, first_in), (turn_c_ref, turn_c_in), (turn_s_ref, turn_s_in),
            (second_ref, second_in), (keeper_ref, keeper_in),
        ])
    ]
    for load in loads + consts:
        load.start()

    barrier = pltpu.get_barrier_semaphore()

    def signal_all(semaphore, there):
        for step in range(n_chan):
            to = lax.rem(chan + step, n_chan)
            pl.semaphore_signal(semaphore, inc=1, device_id=(there, to), device_id_type=MESH)

    def enter(d, carry):
        @pl.when(d > stn)
        def _():
            signal_all(barrier, stn - d + n_stn)

        @pl.when(stn + d < n_stn)
        def _():
            signal_all(barrier, stn + d)

        return carry

    lax.fori_loop(1, half + 1, enter, 0)
    for step in range(1, n_chan):
        there = (stn, lax.rem(chan + step, n_chan))
        pl.semaphore_signal(barrier, inc=1, device_id=there, device_id_type=MESH)

    make_taps(taps_in)
    for c in range(CHUNKS):
        loads[c].wait()
        filter_rows(x_in, taps_in, held, c * rows, rows, inputs, frames)
    for load in consts:
        load.wait()
    planes = transform(held, first_in, turn_c_in, turn_s_in, second_in, inputs * frames)
    for i in range(inputs):
        for f in range(frames):
            for p in range(2):
                plane = planes[i * frames + f][p].astype(jnp.bfloat16)
                for d in range(n_chan):
                    mine[d, i, f, p] = plane[d * tiles : (d + 1) * tiles]
    parts[0, chan] = mine[chan]

    def target(step):
        core = lax.rem(chan, 2)
        return 2 * (step // 2) + lax.rem(core + step, 2)

    def direct(d, step):
        to = target(step)
        return pltpu.make_async_remote_copy(
            src_ref=mine.at[to],
            dst_ref=parts.at[d, chan],
            send_sem=send_sem.at[d, step],
            recv_sem=recv_sem.at[d, chan],
            device_id=(lax.rem(stn + d, n_stn), to),
            device_id_type=MESH,
        )

    def passed(d, origin):
        return pltpu.make_async_remote_copy(
            src_ref=parts.at[d, origin],
            dst_ref=parts.at[d + 1 - 2 * odd, origin],
            send_sem=pass_sem.at[d, origin],
            recv_sem=recv_sem.at[d + 1 - 2 * odd, origin],
            device_id=(pair, chan),
            device_id_type=MESH,
        )

    def passes(d, origin):
        later = d + 1 - 2 * odd
        source = lax.rem(stn + n_stn - d, n_stn)
        needed = (d > 0) & (later > 0) & (later <= half)
        return needed & straight(source, origin, d, n_stn) & ~straight(source, origin, later, n_stn)

    def late(d):
        return stn + d >= n_stn + LAST

    def send(d, carry):
        @pl.when((stn + d >= n_stn) & ~late(d) & straight(stn, chan, d, n_stn))
        def _():
            for step in range(n_chan):
                direct(d, step).start()

        return carry

    def gates(d):
        return (stn + half >= n_stn + LAST) & (stn + d >= n_stn) & ~late(d) & straight(stn, chan, d, n_stn)

    def gate(d, carry):
        @pl.when(gates(d))
        def _():
            direct(d, GATE).wait_send()

        return carry

    def send_late(d, carry):
        @pl.when(late(d) & straight(stn, chan, d, n_stn))
        def _():
            for step in range(n_chan):
                direct(d, step).start()

        return carry

    def send_ahead(d, carry):
        @pl.when(stn + d < n_stn)
        def _():
            pl.semaphore_wait(here_sem.at[d], 1)

            @pl.when(straight(stn, chan, d, n_stn))
            def _():
                for step in range(n_chan):
                    direct(d, step).start()

        return carry

    back = jnp.maximum(stn - half + 1, 0)
    pl.semaphore_wait(barrier, (back + jnp.minimum(stn, half) + 1) * n_chan - 1)


    def answer(d, carry):
        @pl.when(d <= stn)
        def _():
            pl.semaphore_signal(here_sem.at[d], inc=1, device_id=(stn - d, chan), device_id_type=MESH)

        return carry

    lax.fori_loop(1, half + 1, answer, 0)
    last = stn + half >= n_stn + LAST

    @pl.when(~last)
    def _():
        lax.fori_loop(1, half + 1, send, 0)

    for step in range(n_chan):
        @pl.when(target(step) != chan)
        def _():
            direct(0, step).start()

    @pl.when(last)
    def _():
        lax.fori_loop(1, half + 1, send, 0)

    lax.fori_loop(1, half + 1, send_ahead, 0)
    lax.fori_loop(1, half + 1, gate, 0)
    lax.fori_loop(1, half + 1, send_late, 0)

    away = lax.rem(stn + half, n_stn)
    row = keeper_in[pl.ds(stn, 1), :]
    column = lax.broadcasted_iota(jnp.int32, row.shape, 1)
    kept = jnp.max(jnp.where(column == away, row, 0), axis=1, keepdims=True)
    kept = jnp.broadcast_to(kept, (group, LANES)) == 1
    base = jnp.where(stn < half, stn + 1, 0)

    ahead = jnp.minimum(stn, half)

    def comes_straight(d, origin):
        return straight(lax.rem(stn + n_stn - d, n_stn), origin, d, n_stn)

    def all_straight(d):
        source = lax.rem(stn + n_stn - d, n_stn)
        mixed = (lax.rem(source, 2) == 1) & (d > stn) & (d > 2)
        return ((lax.rem(d, 2) == 0) & ~mixed) | ((lax.rem(source, 2) == 0) & (d == 1))

    def rank(d):
        place = jnp.where(d <= ahead, d, half + 1 + ahead - d)
        return jnp.where(all_straight(d), place, place + slots)

    def at_rank(k):
        return jnp.where(k <= ahead, k, half + 1 + ahead - k)

    def receive(k, carry):
        d = at_rank(lax.rem(k, slots))
        for origin in range(n_chan):
            here = (d == 0) & (origin == chan)

            @pl.when((comes_straight(d, origin) == (k < slots)) & ~here)
            def _():
                pltpu.make_async_remote_copy(
                    src_ref=mine.at[0],
                    dst_ref=parts.at[d, origin],
                    send_sem=send_sem.at[0, 0],
                    recv_sem=recv_sem.at[d, origin],
                    device_id=(pair, chan),
                    device_id_type=MESH,
                ).wait_recv()

            @pl.when((k < slots) & passes(d, origin))
            def _():
                passed(d, origin).start()

        @pl.when(all_straight(d) == (k < slots))
        def _():
            take(k, d)

        return carry

    def take(k, d):
        for f in range(frames):
            for p in range(2):
                value = parts[d, :, :, f, p].astype(jnp.float32).reshape(group, tiles, LANES)
                others[d, f, p] = jnp.transpose(value, (1, 0, 2))

        @pl.when(k == 0)
        def _():
            for f in range(frames):
                for p in range(2):
                    own[f, p] = others[0, f, p] * (1.0 / frames)

        def slot(s, inner):
            single = s < base
            with_far = jnp.where(single, stn - s, half + base - s)
            unfilled = (s == half) & ~single
            without = jnp.where(single | unfilled, with_far, with_far - 1)
            gain = jnp.where(unfilled, 0.0, 1.0).astype(jnp.float32)
            ready = jnp.maximum(rank(with_far), rank(without))

            @pl.when(ready == k)
            def _():
                for t in range(tiles):
                    block = [
                        [jnp.where(kept, others[with_far, f, p, t], others[without, f, p, t] * gain) for p in range(2)]
                        for f in range(frames)
                    ]
                    for i in range(group):
                        real, imag = 0.0, 0.0
                        for f in range(frames):
                            a_re, a_im = [jnp.broadcast_to(own[f, p, t, pl.ds(i, 1), :], (group, LANES)) for p in range(2)]
                            b_re, b_im = block[f]
                            real = real + (a_re * b_re + a_im * b_im)
                            imag = imag + (a_im * b_re - a_re * b_im)
                        lanes = slice(t * LANES, (t + 1) * LANES)
                        out_ref[i, 0, s, :, lanes] = real.astype(jnp.bfloat16)
                        out_ref[i, 1, s, :, lanes] = imag.astype(jnp.bfloat16)

            return inner

        lax.fori_loop(0, slots, slot, 0)

    def sent(d, carry):
        @pl.when(straight(stn, chan, d, n_stn))
        def _():
            for step in range(n_chan):
                if step != GATE:
                    direct(d, step).wait_send()

        @pl.when(straight(stn, chan, d, n_stn) & ~gates(d))
        def _():
            direct(d, GATE).wait_send()

        return carry

    def passed_on(d, carry):
        for origin in range(n_chan):
            @pl.when(passes(d, origin))
            def _():
                passed(d, origin).wait_send()

        return carry

    lax.fori_loop(0, slots, receive, 0)
    lax.fori_loop(1, half + 1, sent, 0)
    for step in range(n_chan):
        @pl.when(target(step) != chan)
        def _():
            direct(0, step).wait_send()
    lax.fori_loop(slots, 2 * slots, receive, 0)
    lax.fori_loop(1, half + 1, passed_on, 0)


def per_device(samples, keeper):
    n_stn, n_chan = lax.axis_size("stn"), lax.axis_size("chan")
    inputs, frames_in, _, nfft = samples.shape
    half = n_stn // 2
    frames = frames_in - TAPS + 1
    tiles = CH_WIN // LANES
    n_1 = nfft // LANES
    group = n_chan * inputs
    consts = tables(nfft, CH_WIN * n_chan // n_1)
    x = samples.reshape(inputs, frames_in, 2, n_1, LANES)
    x = jnp.transpose(x, (0, 1, 3, 2, 4)).reshape(inputs, frames_in, 2 * n_1, LANES)
    piece = (n_chan, inputs, frames, 2, tiles, LANES)
    dma = pltpu.SemaphoreType.DMA
    out = pl.pallas_call(
        kernel,
        out_shape=jax.ShapeDtypeStruct((group, 2, half + 1, group, tiles * LANES), jnp.bfloat16),
        in_specs=[pl.BlockSpec(memory_space=pltpu.HBM)] * 6,
        out_specs=pl.BlockSpec(memory_space=pltpu.VMEM),
        scratch_shapes=[
            pltpu.VMEM(x.shape, x.dtype),
            pltpu.VMEM((TAPS, 2 * n_1, LANES), jnp.float32),
            *[pltpu.VMEM(a.shape, a.dtype) for a in consts],
            pltpu.VMEM(keeper.shape, keeper.dtype),
            pltpu.VMEM((2, 2 * n_1, inputs * frames * LANES), jnp.bfloat16),
            pltpu.VMEM(piece, jnp.bfloat16),
            pltpu.VMEM((half + 1,) + piece, jnp.bfloat16),
            pltpu.VMEM((frames, 2, tiles, group, LANES), jnp.float32),
            pltpu.VMEM((half + 1, frames, 2, tiles, group, LANES), jnp.float32),
            dma((CHUNKS,)),
            dma((5,)),
            dma((half + 1, n_chan)),
            dma((half + 1, n_chan)),
            dma((half + 1, n_chan)),
            pltpu.SemaphoreType.REGULAR((half + 1,)),
        ],
        compiler_params=pltpu.CompilerParams(collective_id=0, has_side_effects=True, vmem_limit_bytes=VMEM_LIMIT),
        name="correlator",
    )(*[pltpu.with_memory_space_constraint(a, pltpu.HBM) for a in (keeper, x, *[jnp.asarray(c) for c in consts])])
    out = out.reshape(group, 2, (half + 1) * group, tiles * LANES)
    return jnp.transpose(out, (0, 1, 3, 2))


def solution(mesh):
    placed = (P(("stn", "chan"), None, None, None), P())
    return jax.shard_map(
        per_device,
        mesh=mesh,
        in_specs=placed,
        out_specs=P("stn", None, "chan", None),
        check_vma=False,
    )
```

```python
import math

import jax
import jax.numpy as jnp
import numpy as np
from jax import lax
from jax.experimental import pallas as pl
from jax.experimental.pallas import tpu as pltpu
from jax.sharding import PartitionSpec as P

TAPS = 16
LANES = 128
CH_WIN = 1024
MESH = pl.DeviceIdType.MESH
VMEM_LIMIT = 24 << 20
CHUNKS = 4


def tables(nfft, n_k2):
    n_1 = nfft // LANES
    k_1 = np.arange(n_1)
    n_2 = np.arange(LANES)
    angle = 2.0 * np.pi * (k_1[:, None] * k_1[None, :] % n_1) / n_1
    cosine, sine = np.cos(angle), np.sin(angle)
    first = np.zeros((2, n_1, n_1, 2))
    first[0, :, :, 0] = cosine
    first[0, :, :, 1] = sine
    first[1, :, :, 0] = -sine
    first[1, :, :, 1] = cosine
    first = first.reshape(2 * n_1, 2 * n_1)
    angle = 2.0 * np.pi * (n_2[:, None] * k_1[None, :] % nfft) / nfft
    scale = 1.0 / math.sqrt(nfft)
    turn_c = np.concatenate([np.cos(angle), np.cos(angle)], axis=1) * scale
    turn_s = np.concatenate([np.sin(angle), -np.sin(angle)], axis=1) * scale
    k_2 = np.concatenate([np.arange(0, n_k2, 2), np.arange(1, n_k2, 2)])
    angle = 2.0 * np.pi * (k_2[:, None] * n_2[None, :] % LANES) / LANES
    second = np.concatenate([np.cos(angle), np.sin(angle)], axis=1)
    first = np.concatenate(halves(first), axis=1)
    second = np.concatenate(halves(second), axis=0)
    return [np.asarray(a, np.float32) for a in (turn_c, turn_s)] + [first, second]


def halves(table):
    high = table.astype(jnp.bfloat16)
    return high, (table - high.astype(np.float64)).astype(jnp.bfloat16)


def series(square, terms):
    total = jnp.full_like(square, terms[-1])
    for term in reversed(terms[:-1]):
        total = total * square + term
    return total


def make_taps(taps_ref):
    rows = taps_ref.shape[1]
    nfft = rows // 2 * LANES
    height = 8
    odd = [(-1) ** q * math.pi ** (2 * q) / math.factorial(2 * q + 1) for q in range(7)]
    turn = 2.0 * math.pi / TAPS
    cosine = [(-1) ** q * turn ** (2 * q) / math.factorial(2 * q) for q in range(5)]
    sine = [(-1) ** q * turn ** (2 * q + 1) / math.factorial(2 * q + 1) for q in range(5)]

    def block(j, carry):
        start = pl.multiple_of(j * height, height)
        row = lax.broadcasted_iota(jnp.int32, (height, LANES), 0) + start
        lane = lax.broadcasted_iota(jnp.int32, (height, LANES), 1)
        u = (lax.div(row, 2) * LANES + lane).astype(jnp.float32) * (1.0 / nfft) + 0.5 / nfft
        near = jnp.minimum(u, 1.0 - u)
        wave = near * series(near * near, odd)
        square = u * u
        cos_u, sin_u = series(square, cosine), u * series(square, sine)
        for t in range(TAPS):
            sign = -1.0 if t % 2 else 1.0
            c, s = math.cos(turn * t) * 0.5 * sign, math.sin(turn * t) * 0.5 * sign
            window = (0.5 * sign - c * cos_u) + s * sin_u
            taps_ref[t, pl.ds(start, height), :] = wave * window / (u + (t - TAPS // 2))
        return carry

    lax.fori_loop(0, rows // height, block, 0)


def filter_rows(x_ref, taps_ref, held, first_row, rows, inputs, frames):
    chunk = 16
    for start in range(first_row, first_row + rows, chunk):
        part = slice(start, start + chunk)
        for i in range(inputs):
            totals = [None] * frames
            for step in range(TAPS + frames - 1):
                value = x_ref[i, step, part, :].astype(jnp.float32)
                for f in range(frames):
                    if 0 <= step - f < TAPS:
                        term = value * taps_ref[step - f, part, :]
                        totals[f] = term if totals[f] is None else totals[f] + term
            for f in range(frames):
                seq = i * frames + f
                for q, half in enumerate(split(totals[f])):
                    held[q, part, seq * LANES : (seq + 1) * LANES] = half


def split(value):
    high = value.astype(jnp.bfloat16)
    return high, (value - high.astype(jnp.float32)).astype(jnp.bfloat16)


def dot(a, b):
    return jnp.dot(a, b, preferred_element_type=jnp.float32)


def transform(held, first_ref, turn_c_ref, turn_s_ref, second_ref, seqs):
    half = LANES // 2
    high = held[0]
    depth = high.shape[0]
    stage = dot(first_ref[...], jnp.concatenate([high, high], axis=0)) + dot(first_ref[:, :depth], held[1])
    lane = lax.broadcasted_iota(jnp.int32, (LANES, LANES), 1)
    sign = jnp.where(lane < half, 1.0, -1.0)
    rows = second_ref.shape[0] // 2
    planes = []
    his = []
    for seq in range(seqs):
        turned = stage[:, seq * LANES : (seq + 1) * LANES].T
        turned = turned * turn_c_ref[...] + pltpu.roll(turned, half, 1) * turn_s_ref[...]
        low = pltpu.roll(turned, half, 1) * sign
        his.append(jnp.concatenate([turned, low], axis=0))
    high, rest = split(jnp.concatenate(his, axis=1))
    product = dot(second_ref[...], high)
    every = product[:rows] + product[rows:] + dot(second_ref[:rows], rest)
    for seq in range(seqs):
        spectra = every[:, seq * LANES : (seq + 1) * LANES]
        tiles = rows // 2
        low_lane = lax.broadcasted_iota(jnp.int32, (tiles, LANES), 1) < half
        even, odd = spectra[:tiles], spectra[tiles:]
        real = jnp.where(low_lane, even, pltpu.roll(odd, half, 1))
        imag = jnp.where(low_lane, pltpu.roll(even, half, 1), odd)
        planes.append((real, imag))
    return planes


GATE = 3
LAST = 2


def straight(source, origin, d, n_stn):
    odd = lax.rem(source, 2) == 1
    odd_d = lax.rem(d, 2) == 1
    to_even = (source + d >= n_stn) & (d > 2) & (lax.rem(origin, 2) == 0)
    return (odd & (odd_d == to_even)) | (~odd & (~odd_d | (d == 1))) | (d == 0)


def kernel(
    keeper_ref, x_ref, turn_c_ref, turn_s_ref, first_ref, second_ref, out_ref,
    x_in, taps_in, turn_c_in, turn_s_in, first_in, second_in, keeper_in,
    held, mine, parts, own, others,
    x_sem, const_sem, send_sem, pass_sem, recv_sem, here_sem,
):
    n_chan, inputs, frames, _, tiles, _ = mine.shape
    n_stn = keeper_ref.shape[0]
    half = parts.shape[0] - 1
    slots = half + 1
    group = n_chan * inputs
    stn = lax.axis_index("stn")
    chan = lax.axis_index("chan")
    odd = lax.rem(stn, 2)
    pair = stn + 1 - 2 * odd
    rows = held.shape[1] // CHUNKS

    loads = []
    for c in range(CHUNKS):
        part = pl.ds(c * rows, rows)
        loads.append(pltpu.make_async_copy(x_ref.at[:, :, part], x_in.at[:, :, part], x_sem.at[c]))
    consts = [
        pltpu.make_async_copy(source, target, const_sem.at[q])
        for q, (source, target) in enumerate([
            (first_ref, first_in), (turn_c_ref, turn_c_in), (turn_s_ref, turn_s_in),
            (second_ref, second_in), (keeper_ref, keeper_in),
        ])
    ]
    for load in loads + consts:
        load.start()

    barrier = pltpu.get_barrier_semaphore()

    def signal_all(semaphore, there):
        for step in range(n_chan):
            to = lax.rem(chan + step, n_chan)
            pl.semaphore_signal(semaphore, inc=1, device_id=(there, to), device_id_type=MESH)

    def enter(d, carry):
        @pl.when(d > stn)
        def _():
            signal_all(barrier, stn - d + n_stn)

        @pl.when(stn + d < n_stn)
        def _():
            signal_all(barrier, stn + d)

        return carry

    lax.fori_loop(1, half + 1, enter, 0)
    for step in range(1, n_chan):
        there = (stn, lax.rem(chan + step, n_chan))
        pl.semaphore_signal(barrier, inc=1, device_id=there, device_id_type=MESH)

    make_taps(taps_in)
    for c in range(CHUNKS):
        loads[c].wait()
        filter_rows(x_in, taps_in, held, c * rows, rows, inputs, frames)
    for load in consts:
        load.wait()
    planes = transform(held, first_in, turn_c_in, turn_s_in, second_in, inputs * frames)
    for i in range(inputs):
        for f in range(frames):
            for p in range(2):
                plane = planes[i * frames + f][p].astype(jnp.bfloat16)
                for d in range(n_chan):
                    mine[d, i, f, p] = plane[d * tiles : (d + 1) * tiles]
    parts[0, chan] = mine[chan]

    def target(step):
        core = lax.rem(chan, 2)
        return 2 * (step // 2) + lax.rem(core + step, 2)

    def direct(d, step):
        to = target(step)
        return pltpu.make_async_remote_copy(
            src_ref=mine.at[to],
            dst_ref=parts.at[d, chan],
            send_sem=send_sem.at[d, step],
            recv_sem=recv_sem.at[d, chan],
            device_id=(lax.rem(stn + d, n_stn), to),
            device_id_type=MESH,
        )

    def arrival(d, origin):
        return pltpu.make_async_remote_copy(
            src_ref=mine.at[0],
            dst_ref=parts.at[d, origin],
            send_sem=send_sem.at[0, 0],
            recv_sem=recv_sem.at[d, origin],
            device_id=(pair, chan),
            device_id_type=MESH,
        )

    def passed(d, origin):
        return pltpu.make_async_remote_copy(
            src_ref=parts.at[d, origin],
            dst_ref=parts.at[d + 1 - 2 * odd, origin],
            send_sem=pass_sem.at[d, origin],
            recv_sem=recv_sem.at[d + 1 - 2 * odd, origin],
            device_id=(pair, chan),
            device_id_type=MESH,
        )

    def passes(d, origin):
        later = d + 1 - 2 * odd
        source = lax.rem(stn + n_stn - d, n_stn)
        needed = (d > 0) & (later > 0) & (later <= half)
        return needed & straight(source, origin, d, n_stn) & ~straight(source, origin, later, n_stn)

    def late(d):
        return stn + d >= n_stn + LAST

    def send(d, carry):
        @pl.when((stn + d >= n_stn) & ~late(d) & straight(stn, chan, d, n_stn))
        def _():
            for step in range(n_chan):
                direct(d, step).start()

        return carry

    def gates(d):
        return (stn + half >= n_stn + LAST) & (stn + d >= n_stn) & ~late(d) & straight(stn, chan, d, n_stn)

    def gate(d, carry):
        @pl.when(gates(d))
        def _():
            direct(d, GATE).wait_send()

        return carry

    def send_late(d, carry):
        @pl.when(late(d) & straight(stn, chan, d, n_stn))
        def _():
            for step in range(n_chan):
                direct(d, step).start()

        return carry

    def send_ahead(d, carry):
        @pl.when(stn + d < n_stn)
        def _():
            pl.semaphore_wait(here_sem.at[d], 1)

            @pl.when(straight(stn, chan, d, n_stn))
            def _():
                for step in range(n_chan):
                    direct(d, step).start()

        return carry

    back = jnp.maximum(stn - half + 1, 0)
    pl.semaphore_wait(barrier, (back + jnp.minimum(stn, half) + 1) * n_chan - 1)


    def answer(d, carry):
        @pl.when(d <= stn)
        def _():
            pl.semaphore_signal(here_sem.at[d], inc=1, device_id=(stn - d, chan), device_id_type=MESH)

        return carry

    lax.fori_loop(1, half + 1, answer, 0)
    last = stn + half >= n_stn + LAST

    @pl.when(~last)
    def _():
        lax.fori_loop(1, half + 1, send, 0)

    for step in range(n_chan):
        @pl.when(target(step) != chan)
        def _():
            direct(0, step).start()

    @pl.when(last)
    def _():
        lax.fori_loop(1, half + 1, send, 0)

    lax.fori_loop(1, half + 1, send_ahead, 0)
    lax.fori_loop(1, half + 1, gate, 0)
    for step in range(1, n_chan):
        arrival(0, lax.rem(chan + step, n_chan)).wait_recv()
    lax.fori_loop(1, half + 1, send_late, 0)

    away = lax.rem(stn + half, n_stn)
    row = keeper_in[pl.ds(stn, 1), :]
    column = lax.broadcasted_iota(jnp.int32, row.shape, 1)
    kept = jnp.max(jnp.where(column == away, row, 0), axis=1, keepdims=True)
    kept = jnp.broadcast_to(kept, (group, LANES)) == 1
    base = jnp.where(stn < half, stn + 1, 0)

    ahead = jnp.minimum(stn, half)

    def comes_straight(d, origin):
        return straight(lax.rem(stn + n_stn - d, n_stn), origin, d, n_stn)

    def all_straight(d):
        source = lax.rem(stn + n_stn - d, n_stn)
        mixed = (lax.rem(source, 2) == 1) & (d > stn) & (d > 2)
        return ((lax.rem(d, 2) == 0) & ~mixed) | ((lax.rem(source, 2) == 0) & (d == 1))

    def rank(d):
        place = jnp.where(d <= ahead, d, half + 1 + ahead - d)
        return jnp.where(all_straight(d), place, place + slots)

    def at_rank(k):
        return jnp.where(k <= ahead, k, half + 1 + ahead - k)

    def receive(k, carry):
        d = at_rank(lax.rem(k, slots))
        straight_now = k < slots
        wanted = [comes_straight(d, core) == straight_now for core in range(2)]
        onward = [straight_now & passes(d, core) for core in range(2)]
        for origin in range(n_chan):
            @pl.when(wanted[origin % 2] & (d > 0))
            def _():
                arrival(d, origin).wait_recv()

            @pl.when(onward[origin % 2])
            def _():
                passed(d, origin).start()

        @pl.when(all_straight(d) == (k < slots))
        def _():
            take(k, d)

        return carry

    def take(k, d):
        for f in range(frames):
            for p in range(2):
                value = parts[d, :, :, f, p].astype(jnp.float32).reshape(group, tiles, LANES)
                others[d, f, p] = jnp.transpose(value, (1, 0, 2))

        @pl.when(k == 0)
        def _():
            for f in range(frames):
                for p in range(2):
                    own[f, p] = others[0, f, p] * (1.0 / frames)

        def slot(q, inner):
            single = d < base
            s = jnp.where(single, stn - d, half + base - d - q)
            with_far = jnp.where(single, d, d + q)
            unfilled = (s == half) & ~single
            without = jnp.where(single | unfilled, with_far, with_far - 1)
            gain = jnp.where(unfilled, 0.0, 1.0).astype(jnp.float32)
            other = jnp.where(q == 0, without, with_far)
            held_slot = jnp.where(single, q == 0, s >= base)

            @pl.when(held_slot & (rank(other) <= k))
            def _():
                for t in range(tiles):
                    block = [
                        [jnp.where(kept, others[with_far, f, p, t], others[without, f, p, t] * gain) for p in range(2)]
                        for f in range(frames)
                    ]
                    for i in range(group):
                        real, imag = 0.0, 0.0
                        for f in range(frames):
                            a_re, a_im = [jnp.broadcast_to(own[f, p, t, pl.ds(i, 1), :], (group, LANES)) for p in range(2)]
                            b_re, b_im = block[f]
                            real = real + (a_re * b_re + a_im * b_im)
                            imag = imag + (a_im * b_re - a_re * b_im)
                        lanes = slice(t * LANES, (t + 1) * LANES)
                        out_ref[i, 0, s, :, lanes] = real.astype(jnp.bfloat16)
                        out_ref[i, 1, s, :, lanes] = imag.astype(jnp.bfloat16)

            return inner

        lax.fori_loop(0, 2, slot, 0)

    def sent(d, carry):
        @pl.when(straight(stn, chan, d, n_stn))
        def _():
            for step in range(n_chan):
                if step != GATE:
                    direct(d, step).wait_send()

        @pl.when(straight(stn, chan, d, n_stn) & ~gates(d))
        def _():
            direct(d, GATE).wait_send()

        return carry

    def passed_on(d, carry):
        for origin in range(n_chan):
            @pl.when(passes(d, origin))
            def _():
                passed(d, origin).wait_send()

        return carry

    lax.fori_loop(0, slots, receive, 0)
    lax.fori_loop(1, half + 1, sent, 0)
    for step in range(n_chan):
        @pl.when(target(step) != chan)
        def _():
            direct(0, step).wait_send()
    lax.fori_loop(slots, 2 * slots, receive, 0)
    lax.fori_loop(1, half + 1, passed_on, 0)


def per_device(samples, keeper):
    n_stn, n_chan = lax.axis_size("stn"), lax.axis_size("chan")
    inputs, frames_in, _, nfft = samples.shape
    half = n_stn // 2
    frames = frames_in - TAPS + 1
    tiles = CH_WIN // LANES
    n_1 = nfft // LANES
    group = n_chan * inputs
    consts = tables(nfft, CH_WIN * n_chan // n_1)
    x = samples.reshape(inputs, frames_in, 2, n_1, LANES)
    x = jnp.transpose(x, (0, 1, 3, 2, 4)).reshape(inputs, frames_in, 2 * n_1, LANES)
    piece = (n_chan, inputs, frames, 2, tiles, LANES)
    dma = pltpu.SemaphoreType.DMA
    out = pl.pallas_call(
        kernel,
        out_shape=jax.ShapeDtypeStruct((group, 2, half + 1, group, tiles * LANES), jnp.bfloat16),
        in_specs=[pl.BlockSpec(memory_space=pltpu.HBM)] * 6,
        out_specs=pl.BlockSpec(memory_space=pltpu.VMEM),
        scratch_shapes=[
            pltpu.VMEM(x.shape, x.dtype),
            pltpu.VMEM((TAPS, 2 * n_1, LANES), jnp.float32),
            *[pltpu.VMEM(a.shape, a.dtype) for a in consts],
            pltpu.VMEM(keeper.shape, keeper.dtype),
            pltpu.VMEM((2, 2 * n_1, inputs * frames * LANES), jnp.bfloat16),
            pltpu.VMEM(piece, jnp.bfloat16),
            pltpu.VMEM((half + 1,) + piece, jnp.bfloat16),
            pltpu.VMEM((frames, 2, tiles, group, LANES), jnp.float32),
            pltpu.VMEM((half + 1, frames, 2, tiles, group, LANES), jnp.float32),
            dma((CHUNKS,)),
            dma((5,)),
            dma((half + 1, n_chan)),
            dma((half + 1, n_chan)),
            dma((half + 1, n_chan)),
            pltpu.SemaphoreType.REGULAR((half + 1,)),
        ],
        compiler_params=pltpu.CompilerParams(collective_id=0, has_side_effects=True, vmem_limit_bytes=VMEM_LIMIT),
        name="correlator",
    )(*[pltpu.with_memory_space_constraint(a, pltpu.HBM) for a in (keeper, x, *[jnp.asarray(c) for c in consts])])
    out = out.reshape(group, 2, (half + 1) * group, tiles * LANES)
    return jnp.transpose(out, (0, 1, 3, 2))


def solution(mesh):
    placed = (P(("stn", "chan"), None, None, None), P())
    return jax.shard_map(
        per_device,
        mesh=mesh,
        in_specs=placed,
        out_specs=P("stn", None, "chan", None),
        check_vma=False,
    )
```

```python
import math

import jax
import jax.numpy as jnp
import numpy as np
from jax import lax
from jax.experimental import pallas as pl
from jax.experimental.pallas import tpu as pltpu
from jax.sharding import PartitionSpec as P

TAPS = 16
LANES = 128
CH_WIN = 1024
MESH = pl.DeviceIdType.MESH
VMEM_LIMIT = 24 << 20
CHUNKS = 4


def tables(nfft, n_k2):
    n_1 = nfft // LANES
    k_1 = np.arange(n_1)
    n_2 = np.arange(LANES)
    angle = 2.0 * np.pi * (k_1[:, None] * k_1[None, :] % n_1) / n_1
    cosine, sine = np.cos(angle), np.sin(angle)
    first = np.zeros((2, n_1, n_1, 2))
    first[0, :, :, 0] = cosine
    first[0, :, :, 1] = sine
    first[1, :, :, 0] = -sine
    first[1, :, :, 1] = cosine
    first = first.reshape(2 * n_1, 2 * n_1)
    angle = 2.0 * np.pi * (n_2[:, None] * k_1[None, :] % nfft) / nfft
    scale = 1.0 / math.sqrt(nfft)
    turn_c = np.concatenate([np.cos(angle), np.cos(angle)], axis=1) * scale
    turn_s = np.concatenate([np.sin(angle), -np.sin(angle)], axis=1) * scale
    k_2 = np.concatenate([np.arange(0, n_k2, 2), np.arange(1, n_k2, 2)])
    angle = 2.0 * np.pi * (k_2[:, None] * n_2[None, :] % LANES) / LANES
    second = np.concatenate([np.cos(angle), np.sin(angle)], axis=1)
    first = np.concatenate(halves(first), axis=1)
    second = np.concatenate(halves(second), axis=0)
    return [np.asarray(a, np.float32) for a in (turn_c, turn_s)] + [first, second]


def halves(table):
    high = table.astype(jnp.bfloat16)
    return high, (table - high.astype(np.float64)).astype(jnp.bfloat16)


def series(square, terms):
    total = jnp.full_like(square, terms[-1])
    for term in reversed(terms[:-1]):
        total = total * square + term
    return total


def make_taps(taps_ref):
    rows = taps_ref.shape[1]
    nfft = rows // 2 * LANES
    height = 8
    odd = [(-1) ** q * math.pi ** (2 * q) / math.factorial(2 * q + 1) for q in range(7)]
    turn = 2.0 * math.pi / TAPS
    cosine = [(-1) ** q * turn ** (2 * q) / math.factorial(2 * q) for q in range(5)]
    sine = [(-1) ** q * turn ** (2 * q + 1) / math.factorial(2 * q + 1) for q in range(5)]

    def block(j, carry):
        start = pl.multiple_of(j * height, height)
        row = lax.broadcasted_iota(jnp.int32, (height, LANES), 0) + start
        lane = lax.broadcasted_iota(jnp.int32, (height, LANES), 1)
        u = (lax.div(row, 2) * LANES + lane).astype(jnp.float32) * (1.0 / nfft) + 0.5 / nfft
        near = jnp.minimum(u, 1.0 - u)
        wave = near * series(near * near, odd)
        square = u * u
        cos_u, sin_u = series(square, cosine), u * series(square, sine)
        for t in range(TAPS):
            sign = -1.0 if t % 2 else 1.0
            c, s = math.cos(turn * t) * 0.5 * sign, math.sin(turn * t) * 0.5 * sign
            window = (0.5 * sign - c * cos_u) + s * sin_u
            taps_ref[t, pl.ds(start, height), :] = wave * window / (u + (t - TAPS // 2))
        return carry

    lax.fori_loop(0, rows // height, block, 0)


def filter_rows(x_ref, taps_ref, held, first_row, rows, inputs, frames):
    chunk = 16
    for start in range(first_row, first_row + rows, chunk):
        part = slice(start, start + chunk)
        for i in range(inputs):
            totals = [None] * frames
            for step in range(TAPS + frames - 1):
                value = x_ref[i, step, part, :].astype(jnp.float32)
                for f in range(frames):
                    if 0 <= step - f < TAPS:
                        term = value * taps_ref[step - f, part, :]
                        totals[f] = term if totals[f] is None else totals[f] + term
            for f in range(frames):
                seq = i * frames + f
                for q, half in enumerate(split(totals[f])):
                    held[q, part, seq * LANES : (seq + 1) * LANES] = half


def split(value):
    high = value.astype(jnp.bfloat16)
    return high, (value - high.astype(jnp.float32)).astype(jnp.bfloat16)


def dot(a, b):
    return jnp.dot(a, b, preferred_element_type=jnp.float32)


def transform(held, first_ref, turn_c_ref, turn_s_ref, second_ref, seqs):
    half = LANES // 2
    high = held[0]
    depth = high.shape[0]
    stage = dot(first_ref[...], jnp.concatenate([high, high], axis=0)) + dot(first_ref[:, :depth], held[1])
    lane = lax.broadcasted_iota(jnp.int32, (LANES, LANES), 1)
    sign = jnp.where(lane < half, 1.0, -1.0)
    rows = second_ref.shape[0] // 2
    planes = []
    his = []
    for seq in range(seqs):
        turned = stage[:, seq * LANES : (seq + 1) * LANES].T
        turned = turned * turn_c_ref[...] + pltpu.roll(turned, half, 1) * turn_s_ref[...]
        low = pltpu.roll(turned, half, 1) * sign
        his.append(jnp.concatenate([turned, low], axis=0))
    high, rest = split(jnp.concatenate(his, axis=1))
    product = dot(second_ref[...], high)
    every = product[:rows] + product[rows:] + dot(second_ref[:rows], rest)
    for seq in range(seqs):
        spectra = every[:, seq * LANES : (seq + 1) * LANES]
        tiles = rows // 2
        low_lane = lax.broadcasted_iota(jnp.int32, (tiles, LANES), 1) < half
        even, odd = spectra[:tiles], spectra[tiles:]
        real = jnp.where(low_lane, even, pltpu.roll(odd, half, 1))
        imag = jnp.where(low_lane, pltpu.roll(even, half, 1), odd)
        planes.append((real, imag))
    return planes


LAST = 2


def straight(source, origin, d):
    odd = lax.rem(source, 2) == 1
    odd_d = lax.rem(d, 2) == 1
    to_even = (d > 2) & (lax.rem(origin, 2) == 0)
    return (odd & (odd_d == to_even)) | (~odd & (~odd_d | (d == 1))) | (d == 0)


def kernel(
    keeper_ref, x_ref, turn_c_ref, turn_s_ref, first_ref, second_ref, out_ref,
    x_in, taps_in, turn_c_in, turn_s_in, first_in, second_in, keeper_in,
    held, mine, parts, own, others,
    x_sem, const_sem, send_sem, pass_sem, recv_sem, here_sem,
):
    n_chan, inputs, frames, _, tiles, _ = mine.shape
    n_stn = keeper_ref.shape[0]
    half = parts.shape[0] - 1
    slots = half + 1
    group = n_chan * inputs
    stn = lax.axis_index("stn")
    chan = lax.axis_index("chan")
    odd = lax.rem(stn, 2)
    pair = stn + 1 - 2 * odd
    rows = held.shape[1] // CHUNKS

    loads = []
    for c in range(CHUNKS):
        part = pl.ds(c * rows, rows)
        loads.append(pltpu.make_async_copy(x_ref.at[:, :, part], x_in.at[:, :, part], x_sem.at[c]))
    consts = [
        pltpu.make_async_copy(source, target, const_sem.at[q])
        for q, (source, target) in enumerate([
            (first_ref, first_in), (turn_c_ref, turn_c_in), (turn_s_ref, turn_s_in),
            (second_ref, second_in), (keeper_ref, keeper_in),
        ])
    ]
    for load in loads + consts:
        load.start()

    barrier = pltpu.get_barrier_semaphore()

    def signal_all(semaphore, there):
        for step in range(n_chan):
            to = lax.rem(chan + step, n_chan)
            pl.semaphore_signal(semaphore, inc=1, device_id=(there, to), device_id_type=MESH)

    def enter(d, carry):
        @pl.when(d > stn)
        def _():
            signal_all(barrier, stn - d + n_stn)

        @pl.when(stn + d < n_stn)
        def _():
            signal_all(barrier, stn + d)

        return carry

    lax.fori_loop(1, half + 1, enter, 0)
    for step in range(1, n_chan):
        there = (stn, lax.rem(chan + step, n_chan))
        pl.semaphore_signal(barrier, inc=1, device_id=there, device_id_type=MESH)

    make_taps(taps_in)
    for c in range(CHUNKS):
        loads[c].wait()
        filter_rows(x_in, taps_in, held, c * rows, rows, inputs, frames)
    for load in consts:
        load.wait()
    planes = transform(held, first_in, turn_c_in, turn_s_in, second_in, inputs * frames)
    for i in range(inputs):
        for f in range(frames):
            for p in range(2):
                plane = planes[i * frames + f][p].astype(jnp.bfloat16)
                for d in range(n_chan):
                    mine[d, i, f, p] = plane[d * tiles : (d + 1) * tiles]
    parts[0, chan] = mine[chan]

    def target(step):
        core = lax.rem(chan, 2)
        return 2 * (step // 2) + lax.rem(core + step, 2)

    def direct(d, step):
        to = target(step)
        return pltpu.make_async_remote_copy(
            src_ref=mine.at[to],
            dst_ref=parts.at[d, chan],
            send_sem=send_sem.at[d, step],
            recv_sem=recv_sem.at[d, chan],
            device_id=(lax.rem(stn + d, n_stn), to),
            device_id_type=MESH,
        )

    def arrival(d, origin):
        return pltpu.make_async_remote_copy(
            src_ref=mine.at[0],
            dst_ref=parts.at[d, origin],
            send_sem=send_sem.at[0, 0],
            recv_sem=recv_sem.at[d, origin],
            device_id=(pair, chan),
            device_id_type=MESH,
        )

    def passed(d, origin):
        return pltpu.make_async_remote_copy(
            src_ref=parts.at[d, origin],
            dst_ref=parts.at[d + 1 - 2 * odd, origin],
            send_sem=pass_sem.at[d, origin],
            recv_sem=recv_sem.at[d + 1 - 2 * odd, origin],
            device_id=(pair, chan),
            device_id_type=MESH,
        )

    def passes(d, core):
        even_d = lax.rem(d, 2) == 0
        far = (d > 2) & (core == 0)
        return (d > 1) & jnp.where(odd == 0, (d < half) & (even_d | far), even_d & ~far)

    def late(d):
        return stn + d >= n_stn + LAST

    def send(d, carry):
        @pl.when((stn + d >= n_stn) & ~late(d) & straight(stn, chan, d))
        def _():
            for step in range(n_chan):
                direct(d, step).start()

        return carry

    def send_late(d, carry):
        @pl.when(late(d) & straight(stn, chan, d))
        def _():
            for step in range(n_chan):
                direct(d, step).start()

        return carry

    def send_ahead(d, carry):
        @pl.when(stn + d < n_stn)
        def _():
            pl.semaphore_wait(here_sem.at[d], 1)

            @pl.when(straight(stn, chan, d))
            def _():
                for step in range(n_chan):
                    direct(d, step).start()

        return carry

    back = jnp.maximum(stn - half + 1, 0)
    pl.semaphore_wait(barrier, (back + jnp.minimum(stn, half) + 1) * n_chan - 1)


    last = stn + half >= n_stn + LAST

    @pl.when(~last)
    def _():
        lax.fori_loop(1, half + 1, send, 0)

    for step in range(n_chan):
        @pl.when(target(step) != chan)
        def _():
            direct(0, step).start()

    @pl.when(last)
    def _():
        lax.fori_loop(1, half + 1, send, 0)

    def answer(d, carry):
        @pl.when(d <= stn)
        def _():
            pl.semaphore_signal(here_sem.at[d], inc=1, device_id=(stn - d, chan), device_id_type=MESH)

        return carry

    lax.fori_loop(1, half + 1, answer, 0)
    lax.fori_loop(1, half + 1, send_ahead, 0)
    for step in range(1, n_chan):
        arrival(0, lax.rem(chan + step, n_chan)).wait_recv()
    lax.fori_loop(1, half + 1, send_late, 0)

    away = lax.rem(stn + half, n_stn)
    row = keeper_in[pl.ds(stn, 1), :]
    column = lax.broadcasted_iota(jnp.int32, row.shape, 1)
    kept = jnp.max(jnp.where(column == away, row, 0), axis=1, keepdims=True)
    kept = jnp.broadcast_to(kept, (group, LANES)) == 1
    base = jnp.where(stn < half, stn + 1, 0)

    ahead = jnp.minimum(stn, half)

    def comes_straight(d, core):
        return straight(stn + d, core, d)

    def all_straight(d):
        return comes_straight(d, 0) & comes_straight(d, 1)

    def rank(d):
        place = jnp.where(d <= ahead, d, half + 1 + ahead - d)
        return jnp.where(all_straight(d), place, place + slots)

    def at_rank(k):
        return jnp.where(k <= ahead, k, half + 1 + ahead - k)

    def receive(k, carry):
        d = at_rank(lax.rem(k, slots))
        straight_now = k < slots
        wanted = [comes_straight(d, core) == straight_now for core in range(2)]
        onward = [straight_now & passes(d, core) for core in range(2)]
        for origin in range(n_chan):
            @pl.when(wanted[origin % 2] & (d > 0))
            def _():
                arrival(d, origin).wait_recv()

            @pl.when(onward[origin % 2])
            def _():
                passed(d, origin).start()

        @pl.when(all_straight(d) == (k < slots))
        def _():
            take(k, d)

        return carry

    def take(k, d):
        for f in range(frames):
            for p in range(2):
                value = parts[d, :, :, f, p].astype(jnp.float32).reshape(group, tiles, LANES)
                others[d, f, p] = jnp.transpose(value, (1, 0, 2))

        @pl.when(k == 0)
        def _():
            for f in range(frames):
                for p in range(2):
                    own[f, p] = others[0, f, p] * (1.0 / frames)

        def slot(q, inner):
            single = d < base
            s = jnp.where(single, stn - d, half + base - d - q)
            with_far = jnp.where(single, d, d + q)
            unfilled = (s == half) & ~single
            without = jnp.where(single | unfilled, with_far, with_far - 1)
            gain = jnp.where(unfilled, 0.0, 1.0).astype(jnp.float32)
            other = jnp.where(q == 0, without, with_far)
            held_slot = jnp.where(single, q == 0, s >= base)

            @pl.when(held_slot & (rank(other) <= k))
            def _():
                for t in range(tiles):
                    block = [
                        [jnp.where(kept, others[with_far, f, p, t], others[without, f, p, t] * gain) for p in range(2)]
                        for f in range(frames)
                    ]
                    for i in range(group):
                        real, imag = 0.0, 0.0
                        for f in range(frames):
                            a_re, a_im = [jnp.broadcast_to(own[f, p, t, pl.ds(i, 1), :], (group, LANES)) for p in range(2)]
                            b_re, b_im = block[f]
                            real = real + (a_re * b_re + a_im * b_im)
                            imag = imag + (a_im * b_re - a_re * b_im)
                        lanes = slice(t * LANES, (t + 1) * LANES)
                        out_ref[i, 0, s, :, lanes] = real.astype(jnp.bfloat16)
                        out_ref[i, 1, s, :, lanes] = imag.astype(jnp.bfloat16)

            return inner

        lax.fori_loop(0, 2, slot, 0)

    def sent(d, carry):
        @pl.when(straight(stn, chan, d))
        def _():
            for step in range(n_chan):
                direct(d, step).wait_send()

        return carry

    def passed_on(d, carry):
        for core in range(2):
            @pl.when(passes(d, core))
            def _():
                for origin in range(core, n_chan, 2):
                    passed(d, origin).wait_send()

        return carry

    lax.fori_loop(0, slots, receive, 0)
    lax.fori_loop(1, half + 1, sent, 0)
    for step in range(n_chan):
        @pl.when(target(step) != chan)
        def _():
            direct(0, step).wait_send()
    lax.fori_loop(slots, 2 * slots, receive, 0)
    lax.fori_loop(1, half + 1, passed_on, 0)


def per_device(samples, keeper):
    n_stn, n_chan = lax.axis_size("stn"), lax.axis_size("chan")
    inputs, frames_in, _, nfft = samples.shape
    half = n_stn // 2
    frames = frames_in - TAPS + 1
    tiles = CH_WIN // LANES
    n_1 = nfft // LANES
    group = n_chan * inputs
    consts = tables(nfft, CH_WIN * n_chan // n_1)
    x = samples.reshape(inputs, frames_in, 2, n_1, LANES)
    x = jnp.transpose(x, (0, 1, 3, 2, 4)).reshape(inputs, frames_in, 2 * n_1, LANES)
    piece = (n_chan, inputs, frames, 2, tiles, LANES)
    dma = pltpu.SemaphoreType.DMA
    out = pl.pallas_call(
        kernel,
        out_shape=jax.ShapeDtypeStruct((group, 2, half + 1, group, tiles * LANES), jnp.bfloat16),
        in_specs=[pl.BlockSpec(memory_space=pltpu.HBM)] * 6,
        out_specs=pl.BlockSpec(memory_space=pltpu.VMEM),
        scratch_shapes=[
            pltpu.VMEM(x.shape, x.dtype),
            pltpu.VMEM((TAPS, 2 * n_1, LANES), jnp.float32),
            *[pltpu.VMEM(a.shape, a.dtype) for a in consts],
            pltpu.VMEM(keeper.shape, keeper.dtype),
            pltpu.VMEM((2, 2 * n_1, inputs * frames * LANES), jnp.bfloat16),
            pltpu.VMEM(piece, jnp.bfloat16),
            pltpu.VMEM((half + 1,) + piece, jnp.bfloat16),
            pltpu.VMEM((frames, 2, tiles, group, LANES), jnp.float32),
            pltpu.VMEM((half + 1, frames, 2, tiles, group, LANES), jnp.float32),
            dma((CHUNKS,)),
            dma((5,)),
            dma((half + 1, n_chan)),
            dma((half + 1, n_chan)),
            dma((half + 1, n_chan)),
            pltpu.SemaphoreType.REGULAR((half + 1,)),
        ],
        compiler_params=pltpu.CompilerParams(collective_id=0, has_side_effects=True, vmem_limit_bytes=VMEM_LIMIT),
        name="correlator",
    )(*[pltpu.with_memory_space_constraint(a, pltpu.HBM) for a in (keeper, x, *[jnp.asarray(c) for c in consts])])
    out = out.reshape(group, 2, (half + 1) * group, tiles * LANES)
    return jnp.transpose(out, (0, 1, 3, 2))


def solution(mesh):
    placed = (P(("stn", "chan"), None, None, None), P())
    return jax.shard_map(
        per_device,
        mesh=mesh,
        in_specs=placed,
        out_specs=P("stn", None, "chan", None),
        check_vma=False,
    )
```

```python
import math

import jax
import jax.numpy as jnp
import numpy as np
from jax import lax
from jax.experimental import pallas as pl
from jax.experimental.pallas import tpu as pltpu
from jax.sharding import PartitionSpec as P

TAPS = 16
LANES = 128
CH_WIN = 1024
MESH = pl.DeviceIdType.MESH
VMEM_LIMIT = 24 << 20
CHUNKS = 4


def tables(nfft, n_k2):
    n_1 = nfft // LANES
    k_1 = np.arange(n_1)
    n_2 = np.arange(LANES)
    angle = 2.0 * np.pi * (k_1[:, None] * k_1[None, :] % n_1) / n_1
    cosine, sine = np.cos(angle), np.sin(angle)
    first = np.zeros((2, n_1, n_1, 2))
    first[0, :, :, 0] = cosine
    first[0, :, :, 1] = sine
    first[1, :, :, 0] = -sine
    first[1, :, :, 1] = cosine
    first = first.reshape(2 * n_1, 2 * n_1)
    angle = 2.0 * np.pi * (n_2[:, None] * k_1[None, :] % nfft) / nfft
    scale = 1.0 / math.sqrt(nfft)
    turn_c = np.concatenate([np.cos(angle), np.cos(angle)], axis=1) * scale
    turn_s = np.concatenate([np.sin(angle), -np.sin(angle)], axis=1) * scale
    k_2 = np.concatenate([np.arange(0, n_k2, 2), np.arange(1, n_k2, 2)])
    angle = 2.0 * np.pi * (k_2[:, None] * n_2[None, :] % LANES) / LANES
    second = np.concatenate([np.cos(angle), np.sin(angle)], axis=1)
    first = np.concatenate(halves(first), axis=1)
    second = np.concatenate(halves(second), axis=0)
    return [np.asarray(a, np.float32) for a in (turn_c, turn_s)] + [first, second]


def halves(table):
    high = table.astype(jnp.bfloat16)
    return high, (table - high.astype(np.float64)).astype(jnp.bfloat16)


def series(square, terms):
    total = jnp.full_like(square, terms[-1])
    for term in reversed(terms[:-1]):
        total = total * square + term
    return total


def make_taps(taps_ref):
    rows = taps_ref.shape[1]
    nfft = rows // 2 * LANES
    height = 8
    odd = [(-1) ** q * math.pi ** (2 * q) / math.factorial(2 * q + 1) for q in range(7)]
    turn = 2.0 * math.pi / TAPS
    cosine = [(-1) ** q * turn ** (2 * q) / math.factorial(2 * q) for q in range(5)]
    sine = [(-1) ** q * turn ** (2 * q + 1) / math.factorial(2 * q + 1) for q in range(5)]

    def block(j, carry):
        start = pl.multiple_of(j * height, height)
        row = lax.broadcasted_iota(jnp.int32, (height, LANES), 0) + start
        lane = lax.broadcasted_iota(jnp.int32, (height, LANES), 1)
        u = (lax.div(row, 2) * LANES + lane).astype(jnp.float32) * (1.0 / nfft) + 0.5 / nfft
        near = jnp.minimum(u, 1.0 - u)
        wave = near * series(near * near, odd)
        square = u * u
        cos_u, sin_u = series(square, cosine), u * series(square, sine)
        for t in range(TAPS):
            sign = -1.0 if t % 2 else 1.0
            c, s = math.cos(turn * t) * 0.5 * sign, math.sin(turn * t) * 0.5 * sign
            window = (0.5 * sign - c * cos_u) + s * sin_u
            taps_ref[t, pl.ds(start, height), :] = wave * window / (u + (t - TAPS // 2))
        return carry

    lax.fori_loop(0, rows // height, block, 0)


def filter_rows(x_ref, taps_ref, held, first_row, rows, inputs, frames):
    chunk = 16
    for start in range(first_row, first_row + rows, chunk):
        part = slice(start, start + chunk)
        for i in range(inputs):
            totals = [None] * frames
            for step in range(TAPS + frames - 1):
                value = x_ref[i, step, part, :].astype(jnp.float32)
                for f in range(frames):
                    if 0 <= step - f < TAPS:
                        term = value * taps_ref[step - f, part, :]
                        totals[f] = term if totals[f] is None else totals[f] + term
            for f in range(frames):
                seq = i * frames + f
                for q, half in enumerate(split(totals[f])):
                    held[q, part, seq * LANES : (seq + 1) * LANES] = half


def split(value):
    high = value.astype(jnp.bfloat16)
    return high, (value - high.astype(jnp.float32)).astype(jnp.bfloat16)


def dot(a, b):
    return jnp.dot(a, b, preferred_element_type=jnp.float32)


def transform(held, first_ref, turn_c_ref, turn_s_ref, second_ref, seqs):
    half = LANES // 2
    high = held[0]
    depth = high.shape[0]
    stage = dot(first_ref[...], jnp.concatenate([high, high], axis=0)) + dot(first_ref[:, :depth], held[1])
    lane = lax.broadcasted_iota(jnp.int32, (LANES, LANES), 1)
    sign = jnp.where(lane < half, 1.0, -1.0)
    rows = second_ref.shape[0] // 2
    planes = []
    his = []
    for seq in range(seqs):
        turned = stage[:, seq * LANES : (seq + 1) * LANES].T
        turned = turned * turn_c_ref[...] + pltpu.roll(turned, half, 1) * turn_s_ref[...]
        low = pltpu.roll(turned, half, 1) * sign
        his.append(jnp.concatenate([turned, low], axis=0))
    high, rest = split(jnp.concatenate(his, axis=1))
    product = dot(second_ref[...], high)
    every = product[:rows] + product[rows:] + dot(second_ref[:rows], rest)
    for seq in range(seqs):
        spectra = every[:, seq * LANES : (seq + 1) * LANES]
        tiles = rows // 2
        low_lane = lax.broadcasted_iota(jnp.int32, (tiles, LANES), 1) < half
        even, odd = spectra[:tiles], spectra[tiles:]
        real = jnp.where(low_lane, even, pltpu.roll(odd, half, 1))
        imag = jnp.where(low_lane, pltpu.roll(even, half, 1), odd)
        planes.append((real, imag))
    return planes


LAST = 2


def straight(source, origin, d):
    odd = lax.rem(source, 2) == 1
    odd_d = lax.rem(d, 2) == 1
    to_even = (d > 2) & (lax.rem(origin, 2) == 0)
    return (odd & (odd_d == to_even)) | (~odd & (~odd_d | (d == 1))) | (d == 0)


def kernel(
    keeper_ref, x_ref, turn_c_ref, turn_s_ref, first_ref, second_ref, out_ref,
    x_in, taps_in, turn_c_in, turn_s_in, first_in, second_in, keeper_in,
    held, mine, parts, own, others,
    x_sem, const_sem, send_sem, pass_sem, recv_sem, here_sem,
):
    n_chan, inputs, frames, _, tiles, _ = mine.shape
    n_stn = keeper_ref.shape[0]
    half = parts.shape[0] - 1
    slots = half + 1
    group = n_chan * inputs
    stn = lax.axis_index("stn")
    chan = lax.axis_index("chan")
    odd = lax.rem(stn, 2)
    pair = stn + 1 - 2 * odd
    rows = held.shape[1] // CHUNKS

    loads = []
    for c in range(CHUNKS):
        part = pl.ds(c * rows, rows)
        loads.append(pltpu.make_async_copy(x_ref.at[:, :, part], x_in.at[:, :, part], x_sem.at[c]))
    consts = [
        pltpu.make_async_copy(source, target, const_sem.at[q])
        for q, (source, target) in enumerate([
            (first_ref, first_in), (turn_c_ref, turn_c_in), (turn_s_ref, turn_s_in),
            (second_ref, second_in), (keeper_ref, keeper_in),
        ])
    ]
    for load in loads + consts:
        load.start()

    barrier = pltpu.get_barrier_semaphore()

    def signal_all(semaphore, there):
        for step in range(n_chan):
            to = lax.rem(chan + step, n_chan)
            pl.semaphore_signal(semaphore, inc=1, device_id=(there, to), device_id_type=MESH)

    def enter(d, carry):
        @pl.when(d > stn)
        def _():
            signal_all(barrier, stn - d + n_stn)

        @pl.when(stn + d < n_stn)
        def _():
            signal_all(barrier, stn + d)

        return carry

    lax.fori_loop(1, half + 1, enter, 0)
    for step in range(1, n_chan):
        there = (stn, lax.rem(chan + step, n_chan))
        pl.semaphore_signal(barrier, inc=1, device_id=there, device_id_type=MESH)

    make_taps(taps_in)
    for c in range(CHUNKS):
        loads[c].wait()
        filter_rows(x_in, taps_in, held, c * rows, rows, inputs, frames)
    for load in consts:
        load.wait()
    planes = transform(held, first_in, turn_c_in, turn_s_in, second_in, inputs * frames)
    for i in range(inputs):
        for f in range(frames):
            for p in range(2):
                plane = planes[i * frames + f][p].astype(jnp.bfloat16)
                for d in range(n_chan):
                    mine[d, i, f, p] = plane[d * tiles : (d + 1) * tiles]
    parts[0, chan] = mine[chan]

    def target(step):
        core = lax.rem(chan, 2)
        return 2 * (step // 2) + lax.rem(core + step, 2)

    def direct(d, step):
        to = target(step)
        return pltpu.make_async_remote_copy(
            src_ref=mine.at[to],
            dst_ref=parts.at[d, chan],
            send_sem=send_sem.at[d, step],
            recv_sem=recv_sem.at[d, chan],
            device_id=(lax.rem(stn + d, n_stn), to),
            device_id_type=MESH,
        )

    def arrival(d, origin):
        return pltpu.make_async_remote_copy(
            src_ref=mine.at[0],
            dst_ref=parts.at[d, origin],
            send_sem=send_sem.at[0, 0],
            recv_sem=recv_sem.at[d, origin],
            device_id=(pair, chan),
            device_id_type=MESH,
        )

    def passed(d, origin):
        return pltpu.make_async_remote_copy(
            src_ref=parts.at[d, origin],
            dst_ref=parts.at[d + 1 - 2 * odd, origin],
            send_sem=pass_sem.at[d, origin],
            recv_sem=recv_sem.at[d + 1 - 2 * odd, origin],
            device_id=(pair, chan),
            device_id_type=MESH,
        )

    def passes(d, core):
        even_d = lax.rem(d, 2) == 0
        far = (d > 2) & (core == 0)
        return (d > 1) & jnp.where(odd == 0, (d < half) & (even_d | far), even_d & ~far)

    def late(d):
        return stn + d >= n_stn + LAST

    def send(d, carry):
        @pl.when((stn + d >= n_stn) & ~late(d) & straight(stn, chan, d))
        def _():
            for step in range(n_chan):
                direct(d, step).start()

        return carry

    def send_late(d, carry):
        @pl.when(late(d) & straight(stn, chan, d))
        def _():
            for step in range(n_chan):
                direct(d, step).start()

        return carry

    def send_ahead(d, carry):
        @pl.when(stn + d < n_stn)
        def _():
            pl.semaphore_wait(here_sem.at[d], 1)

            @pl.when(straight(stn, chan, d))
            def _():
                for step in range(n_chan):
                    direct(d, step).start()

        return carry

    back = jnp.maximum(stn - half + 1, 0)
    pl.semaphore_wait(barrier, (back + jnp.minimum(stn, half) + 1) * n_chan - 1)


    for step in range(n_chan):
        @pl.when(target(step) != chan)
        def _():
            direct(0, step).start()

    lax.fori_loop(1, half + 1, send, 0)

    def answer(d, carry):
        @pl.when(d <= stn)
        def _():
            pl.semaphore_signal(here_sem.at[d], inc=1, device_id=(stn - d, chan), device_id_type=MESH)

        return carry

    lax.fori_loop(1, half + 1, answer, 0)
    lax.fori_loop(1, half + 1, send_ahead, 0)
    for step in range(1, n_chan):
        arrival(0, lax.rem(chan + step, n_chan)).wait_recv()
    lax.fori_loop(1, half + 1, send_late, 0)

    away = lax.rem(stn + half, n_stn)
    row = keeper_in[pl.ds(stn, 1), :]
    column = lax.broadcasted_iota(jnp.int32, row.shape, 1)
    kept = jnp.max(jnp.where(column == away, row, 0), axis=1, keepdims=True)
    kept = jnp.broadcast_to(kept, (group, LANES)) == 1
    base = jnp.where(stn < half, stn + 1, 0)

    ahead = jnp.minimum(stn, half)

    def comes_straight(d, core):
        return straight(stn + d, core, d)

    def all_straight(d):
        return comes_straight(d, 0) & comes_straight(d, 1)

    def rank(d):
        place = jnp.where(d <= ahead, d, half + 1 + ahead - d)
        return jnp.where(all_straight(d), place, place + slots)

    def at_rank(k):
        return jnp.where(k <= ahead, k, half + 1 + ahead - k)

    def receive(k, carry):
        d = at_rank(lax.rem(k, slots))
        straight_now = k < slots
        wanted = [comes_straight(d, core) == straight_now for core in range(2)]
        onward = [straight_now & passes(d, core) for core in range(2)]
        for origin in range(n_chan):
            @pl.when(wanted[origin % 2] & (d > 0))
            def _():
                arrival(d, origin).wait_recv()

            @pl.when(onward[origin % 2])
            def _():
                passed(d, origin).start()

        @pl.when(all_straight(d) == (k < slots))
        def _():
            take(k, d)

        return carry

    def take(k, d):
        for f in range(frames):
            for p in range(2):
                value = parts[d, :, :, f, p].astype(jnp.float32).reshape(group, tiles, LANES)
                others[d, f, p] = jnp.transpose(value, (1, 0, 2))

        @pl.when(k == 0)
        def _():
            for f in range(frames):
                for p in range(2):
                    own[f, p] = others[0, f, p] * (1.0 / frames)

        def slot(q, inner):
            single = d < base
            s = jnp.where(single, stn - d, half + base - d - q)
            with_far = jnp.where(single, d, d + q)
            unfilled = (s == half) & ~single
            without = jnp.where(single | unfilled, with_far, with_far - 1)
            gain = jnp.where(unfilled, 0.0, 1.0).astype(jnp.float32)
            other = jnp.where(q == 0, without, with_far)
            held_slot = jnp.where(single, q == 0, s >= base)

            @pl.when(held_slot & (rank(other) <= k))
            def _():
                for t in range(tiles):
                    block = [
                        [jnp.where(kept, others[with_far, f, p, t], others[without, f, p, t] * gain) for p in range(2)]
                        for f in range(frames)
                    ]
                    for i in range(group):
                        real, imag = 0.0, 0.0
                        for f in range(frames):
                            a_re, a_im = [jnp.broadcast_to(own[f, p, t, pl.ds(i, 1), :], (group, LANES)) for p in range(2)]
                            b_re, b_im = block[f]
                            real = real + (a_re * b_re + a_im * b_im)
                            imag = imag + (a_im * b_re - a_re * b_im)
                        lanes = slice(t * LANES, (t + 1) * LANES)
                        out_ref[i, 0, s, :, lanes] = real.astype(jnp.bfloat16)
                        out_ref[i, 1, s, :, lanes] = imag.astype(jnp.bfloat16)

            return inner

        lax.fori_loop(0, 2, slot, 0)

    def sent(d, carry):
        @pl.when(straight(stn, chan, d))
        def _():
            for step in range(n_chan):
                direct(d, step).wait_send()

        return carry

    def passed_on(d, carry):
        for core in range(2):
            @pl.when(passes(d, core))
            def _():
                for origin in range(core, n_chan, 2):
                    passed(d, origin).wait_send()

        return carry

    lax.fori_loop(0, slots, receive, 0)
    lax.fori_loop(1, half + 1, sent, 0)
    for step in range(n_chan):
        @pl.when(target(step) != chan)
        def _():
            direct(0, step).wait_send()
    lax.fori_loop(slots, 2 * slots, receive, 0)
    lax.fori_loop(1, half + 1, passed_on, 0)


def per_device(samples, keeper):
    n_stn, n_chan = lax.axis_size("stn"), lax.axis_size("chan")
    inputs, frames_in, _, nfft = samples.shape
    half = n_stn // 2
    frames = frames_in - TAPS + 1
    tiles = CH_WIN // LANES
    n_1 = nfft // LANES
    group = n_chan * inputs
    consts = tables(nfft, CH_WIN * n_chan // n_1)
    x = samples.reshape(inputs, frames_in, 2, n_1, LANES)
    x = jnp.transpose(x, (0, 1, 3, 2, 4)).reshape(inputs, frames_in, 2 * n_1, LANES)
    piece = (n_chan, inputs, frames, 2, tiles, LANES)
    dma = pltpu.SemaphoreType.DMA
    out = pl.pallas_call(
        kernel,
        out_shape=jax.ShapeDtypeStruct((group, 2, half + 1, group, tiles * LANES), jnp.bfloat16),
        in_specs=[pl.BlockSpec(memory_space=pltpu.HBM)] * 6,
        out_specs=pl.BlockSpec(memory_space=pltpu.VMEM),
        scratch_shapes=[
            pltpu.VMEM(x.shape, x.dtype),
            pltpu.VMEM((TAPS, 2 * n_1, LANES), jnp.float32),
            *[pltpu.VMEM(a.shape, a.dtype) for a in consts],
            pltpu.VMEM(keeper.shape, keeper.dtype),
            pltpu.VMEM((2, 2 * n_1, inputs * frames * LANES), jnp.bfloat16),
            pltpu.VMEM(piece, jnp.bfloat16),
            pltpu.VMEM((half + 1,) + piece, jnp.bfloat16),
            pltpu.VMEM((frames, 2, tiles, group, LANES), jnp.float32),
            pltpu.VMEM((half + 1, frames, 2, tiles, group, LANES), jnp.float32),
            dma((CHUNKS,)),
            dma((5,)),
            dma((half + 1, n_chan)),
            dma((half + 1, n_chan)),
            dma((half + 1, n_chan)),
            pltpu.SemaphoreType.REGULAR((half + 1,)),
        ],
        compiler_params=pltpu.CompilerParams(collective_id=0, has_side_effects=True, vmem_limit_bytes=VMEM_LIMIT),
        name="correlator",
    )(*[pltpu.with_memory_space_constraint(a, pltpu.HBM) for a in (keeper, x, *[jnp.asarray(c) for c in consts])])
    out = out.reshape(group, 2, (half + 1) * group, tiles * LANES)
    return jnp.transpose(out, (0, 1, 3, 2))


def solution(mesh):
    placed = (P(("stn", "chan"), None, None, None), P())
    return jax.shard_map(
        per_device,
        mesh=mesh,
        in_specs=placed,
        out_specs=P("stn", None, "chan", None),
        check_vma=False,
    )
```
